32 devices in a mesh: grp: 2 (over y), blk: 8 (over z, x), tp: 2 (over core).
Axes of the slice: x: 2, y: 2, z: 4, core: 2. Of those that a mesh axis runs over, the one named last changes fastest.
Arguments:
- hidden_in: bfloat16 [2048, 2048], P(('grp', 'blk'), 'tp'), may hold values from -6 to 6
- norm_gain: float32 [2048], replicated, may hold values from 0.1 to 1.9
- w_qkv: bfloat16 [2048, 3, 2048], P(None, None, 'tp'), may hold values from -0.15467961 to 0.15467961
- w_out: bfloat16 [2048, 2048], P('tp'), may hold values from -0.125 to 0.125
- prefix_kv: bfloat16 [1024, 2, 2048], P(('grp', 'blk'), None, 'tp'), may hold values from -6 to 6
- segment: int32 [2, 1024], P('grp', 'blk'), may hold values from 0 to 7, never falling along the last dimension, each value on 1 to 640 neighbouring positions
Outputs:
- attended: bfloat16 [2048, 2048], P(('grp', 'blk', 'tp'))
- keys_values: bfloat16 [2048, 2, 2048], P(('grp', 'blk'), None, 'tp')
The draws below stay inside these ranges and needn't reach their ends.
Inputs may be any that keep to these rules, and one draw needn't show every extreme that they name: `segment`: within each row the request numbers never fall; each request has 1 to 640 tokens, and one has exactly 640.
All inputs are finite; a program needn't handle non-finite values.
Results may differ from the reference program's by a relative error of at most 0.011.
Values may be sent and summed in bfloat16 or wider, within the bound.
A program may use at most 128 MiB of HBM per device.

```python
import math
import jax
import jax.numpy as jnp
import numpy as np
from jax import lax

D = 2048
HEADS = 32
HD = 64
REQS = 8
GTOK = 1024
TOKENS = 2048
PREFIX = 1024
MOST = 640
N_GRP = 2
N_TP = 2


def shared_signs(key):
    half_signs = jax.random.randint(jax.random.fold_in(key, 4242), (D // 2,), 0, 2).astype(jnp.float32) * 2.0 - 1.0
    return jnp.concatenate([half_signs, -half_signs])


def draw_hidden_in(key, part):
    sign_row = shared_signs(key)
    jitter_key = jax.random.fold_in(key, 11)
    level_key = jax.random.fold_in(key, 12)
    jitter = jnp.clip(jax.random.normal(jitter_key, (TOKENS, D), jnp.float32), -2.0, 2.0)
    levels = jnp.maximum(jax.random.uniform(level_key, (TOKENS, 1), jnp.float32, -4.0, 4.0), 0.0)
    return (jitter + levels * sign_row[None, :]).astype(jnp.bfloat16)


def draw_w_qkv(key, part):
    sign_row = shared_signs(key)
    random_key = jax.random.fold_in(key, 21)
    random_part = jnp.clip(jax.random.normal(random_key, (D, 3, D), jnp.float32), -6.0, 6.0)
    strength = 48.0
    column = jnp.arange(D, dtype=jnp.int32)
    head_of = column // HD
    within_head = column % HD
    aligned = jnp.where((head_of % 4 == 0) & (within_head >= HD // 4), 1.0, 0.0) / math.sqrt(HD - HD // 4)
    which_part = jnp.arange(3, dtype=jnp.int32)
    part_mask = jnp.where(which_part < 2, 1.0, 0.0)
    aligned_part = strength / D * sign_row[:, None, None] * part_mask[None, :, None] * aligned[None, None, :]
    return (random_part / math.sqrt(D) + aligned_part).astype(jnp.bfloat16)


def block_levels(stream_key, extent, pieces, least, top_value):
    def one(position, shards_of):
        steps = jax.random.uniform(jax.random.fold_in(jax.random.fold_in(stream_key, 6), position), (shards_of,), jnp.float32, least / len(pieces), top_value / len(pieces))
        return jnp.repeat(jnp.exp(steps), extent[position] // shards_of).reshape((-1,) + (1,) * (len(extent) - position - 1))

    factor_of = one(*pieces[0])
    for cut in pieces[1:]:
        factor_of = factor_of * one(*cut)
    return factor_of


def split_up(amount, total, most, skew):
    portions = [(1 << 20) // math.isqrt(rank ** skew) + 1 for rank in range(2, amount + 1)]
    spare, holding = total - most - (amount - 1), [1] * (amount - 1)
    while spare > 0:
        candidates = [i for i in range(amount - 1) if holding[i] < most]
        pool, budget = sum([portions[i] for i in candidates]), spare
        for i in candidates:
            more = min(most - holding[i], max(1, budget * portions[i] // pool), spare)
            holding[i] = holding[i] + more
            spare = spare - more
    return np.array([most] + holding)


def ragged(key, count, total, most, slope):
    if count == 2:
        one = jax.random.randint(key, (), max(1, total - most), min(most, total - 1) + 1)
        return jnp.stack([one, total - one])
    lengths = jnp.asarray(split_up(count, total, most, slope), jnp.int32)
    couples = (count - 1) // 2
    giver, receiver = lengths[1:1 + 2 * couples:2], lengths[2:2 + 2 * couples:2]
    room = jnp.minimum(giver - 1, most - receiver)
    passed = jax.random.randint(jax.random.fold_in(key, 1), (couples,), 0, 1 << 20) % (room + 1)
    lengths = lengths.at[1:1 + 2 * couples:2].set(giver - passed).at[2:2 + 2 * couples:2].set(receiver + passed)
    return lengths[jax.random.permutation(jax.random.fold_in(key, 2), count)]


def normal_values(key, extent, width, reach, pieces=(), held_as=jnp.bfloat16):
    factor_of = block_levels(key, extent, pieces, -0.22, 0.18) if pieces else 1.0
    values = jax.random.normal(key, extent, jnp.float32) * width * factor_of
    return jnp.minimum(jnp.maximum(values, -reach), reach).astype(held_as)


def setup_inputs(seed: int = 0) -> dict:
    keys = jax.random.split(jax.random.key(seed), 7)
    hidden_in = draw_hidden_in(jax.random.fold_in(keys[6], 71), 0)
    norm_gain = jnp.clip(1.0 + 0.18 * jax.random.normal(keys[1], (D,), jnp.float32), 0.1, 1.9)
    w_qkv = draw_w_qkv(jax.random.fold_in(keys[6], 71), 0)
    w_out = normal_values(keys[3], (D, D), D ** -0.5, 0.125, ((0, 2),))
    prefix_kv = normal_values(keys[4], (PREFIX, 2, D), 1.0, 6.0, ((0, 16), (2, 2)))
    segment = jax.vmap(lambda own: jnp.searchsorted(jnp.cumsum(ragged(own, REQS, GTOK, MOST, 2)), jnp.arange(GTOK), side="right"))(jax.random.split(keys[5], N_GRP)).reshape((N_GRP, GTOK)).astype(jnp.int32)
    return {"hidden_in": hidden_in, "norm_gain": norm_gain, "w_qkv": w_qkv, "w_out": w_out, "prefix_kv": prefix_kv, "segment": segment}


def layer_norm(matrix_rows, norm_gain):
    values_f = matrix_rows.astype(jnp.float32)
    row_mean = lax.optimization_barrier(jnp.mean(values_f, axis=-1, keepdims=True))
    centered = values_f - row_mean
    variance = lax.optimization_barrier(jnp.mean(centered * centered, axis=-1, keepdims=True))
    return (centered * lax.rsqrt(variance + 1e-05) * norm_gain.astype(jnp.float32)).astype(jnp.bfloat16)

def rotary(heads_f, positions):
    head_size = heads_f.shape[-1]
    rotated = head_size // 4
    half_rot = rotated // 2
    inverse = 10000.0 ** (-(jnp.arange(half_rot, dtype=jnp.float32) * 2.0) / rotated)
    angles = positions[:, None] * inverse[None, :]
    cos_table = jnp.cos(angles)[:, None, :]
    sine_table = jnp.sin(angles)[:, None, :]
    first_half = heads_f[..., :half_rot]
    second_half = heads_f[..., half_rot:rotated]
    return jnp.concatenate([first_half * cos_table - second_half * sine_table, second_half * cos_table + first_half * sine_table, heads_f[..., rotated:]], axis=-1)

def positions_of(segment_row, prefix_len):
    onehot = (segment_row[:, None] == jnp.arange(REQS, dtype=jnp.int32)[None, :]).astype(jnp.int32)
    counts = lax.optimization_barrier(jnp.sum(onehot, axis=0))
    starts = jnp.cumsum(counts) - counts
    token_index = jnp.arange(segment_row.shape[0], dtype=jnp.int32)
    within = token_index - lax.optimization_barrier(jnp.sum(onehot * starts[None, :], axis=1))
    return within.astype(jnp.float32) + prefix_len

def reference(hidden_in, norm_gain, w_qkv, w_out, prefix_kv, segment):
    model_width = hidden_in.shape[1]
    prefix_len = prefix_kv.shape[0]
    pre_keys = prefix_kv[:, 0].reshape(prefix_len, HEADS, HD).astype(jnp.float32)
    pre_values = prefix_kv[:, 1].reshape(prefix_len, HEADS, HD).astype(jnp.float32)
    score_scale = 1.0 / math.sqrt(HD)
    block_size = math.gcd(GTOK, 256)
    block_total = GTOK // block_size
    share_width = model_width // N_TP
    attended_parts = []
    stacked_parts = []
    for group_index in range(N_GRP):
        group_rows = hidden_in[group_index * GTOK:(group_index + 1) * GTOK]
        normed = layer_norm(group_rows, norm_gain)
        projected = jnp.dot(normed, w_qkv.reshape(model_width, 3 * model_width), preferred_element_type=jnp.float32).reshape(GTOK, 3, HEADS, HD)
        seg_row = segment[group_index]
        positions = positions_of(seg_row, float(prefix_len))
        queries = rotary(projected[:, 0], positions).astype(jnp.bfloat16)
        key_heads = rotary(projected[:, 1], positions).astype(jnp.bfloat16)
        values = projected[:, 2].astype(jnp.bfloat16)
        stacked_parts.append(jnp.stack([key_heads.reshape(GTOK, model_width), values.reshape(GTOK, model_width)], axis=1))
        key_f = key_heads.astype(jnp.float32)
        value_f = values.astype(jnp.float32)
        token_index = jnp.arange(GTOK, dtype=jnp.int32)

        def one_block(block_number):
            first_row = (block_number * block_size).astype(jnp.int32)
            query_blk = lax.dynamic_slice_in_dim(queries, first_row, block_size, 0).astype(jnp.float32)
            seg_blk = lax.dynamic_slice_in_dim(seg_row, first_row, block_size, 0)
            index_blk = first_row + jnp.arange(block_size, dtype=jnp.int32)
            pre_scores = jnp.einsum('qhd,khd->qhk', query_blk, pre_keys) * score_scale
            suf_scores = jnp.einsum('qhd,khd->qhk', query_blk, key_f) * score_scale
            visible = (seg_blk[:, None] == seg_row[None, :]) & (token_index[None, :] <= index_blk[:, None])
            suf_scores = jnp.where(visible[:, None, :], suf_scores, jnp.float32(-1e+30))
            row_top = jnp.maximum(lax.optimization_barrier(jnp.max(pre_scores, axis=-1)), lax.optimization_barrier(jnp.max(suf_scores, axis=-1)))
            pre_weights = jnp.exp(pre_scores - row_top[..., None])
            suf_weights = jnp.where(visible[:, None, :], jnp.exp(suf_scores - row_top[..., None]), jnp.float32(0.0))
            denominator = lax.optimization_barrier(jnp.sum(pre_weights, axis=-1)) + lax.optimization_barrier(jnp.sum(suf_weights, axis=-1))
            pre_rounded = lax.optimization_barrier(pre_weights.astype(jnp.bfloat16)).astype(jnp.float32)
            suf_rounded = lax.optimization_barrier(suf_weights.astype(jnp.bfloat16)).astype(jnp.float32)
            combined = jnp.einsum('qhk,khd->qhd', pre_rounded, pre_values) + jnp.einsum('qhk,khd->qhd', suf_rounded, value_f)
            return (combined / denominator[..., None]).astype(jnp.bfloat16).reshape(block_size, model_width)
        attention = lax.map(one_block, jnp.arange(block_total, dtype=jnp.int32)).reshape(GTOK, model_width)
        summed = jnp.zeros((GTOK, model_width), jnp.float32)
        for share_index in range(N_TP):
            first_col = share_index * share_width
            partial_value = jnp.dot(attention[:, first_col:first_col + share_width], w_out[first_col:first_col + share_width], preferred_element_type=jnp.float32)
            summed = summed + lax.optimization_barrier(partial_value.astype(jnp.bfloat16)).astype(jnp.float32)
        attended_parts.append(summed.astype(jnp.bfloat16))
    return (jnp.concatenate(attended_parts, axis=0), jnp.concatenate(stacked_parts, axis=0))
```

```python
import math

import jax
import jax.numpy as jnp
import numpy as np
from jax import lax
from jax.experimental import pallas as pl
from jax.experimental.pallas import tpu as pltpu
from jax.sharding import PartitionSpec as P

HD = 64
REQS = 8


def layer_norm(matrix_rows, norm_gain):
    values_f = matrix_rows.astype(jnp.float32)
    row_mean = jnp.mean(values_f, axis=-1, keepdims=True)
    centered = values_f - row_mean
    variance = jnp.mean(centered * centered, axis=-1, keepdims=True)
    return (centered * lax.rsqrt(variance + 1e-05) * norm_gain).astype(jnp.bfloat16)


def rotary(heads_f, positions):
    head_size = heads_f.shape[-1]
    rotated = head_size // 4
    half_rot = rotated // 2
    inverse = 10000.0 ** (-(jnp.arange(half_rot, dtype=jnp.float32) * 2.0) / rotated)
    angles = positions[:, None] * inverse[None, :]
    cos_table = jnp.cos(angles)[:, None, :]
    sine_table = jnp.sin(angles)[:, None, :]
    first_half = heads_f[..., :half_rot]
    second_half = heads_f[..., half_rot:rotated]
    return jnp.concatenate(
        [
            first_half * cos_table - second_half * sine_table,
            second_half * cos_table + first_half * sine_table,
            heads_f[..., rotated:],
        ],
        axis=-1,
    )


def attend_block(carried, queries, block_kv, visible, score_scale):
    maxima, totals, accumulated = carried
    key_count = block_kv.shape[0]
    head_count = queries.shape[1]
    block_keys = block_kv[:, 0].reshape(key_count, head_count, HD)
    block_values = block_kv[:, 1].reshape(key_count, head_count, HD)
    scores = (
        jnp.einsum("qhd,khd->qhk", queries, block_keys, preferred_element_type=jnp.float32)
        * score_scale
    )
    if visible is not None:
        scores = jnp.where(visible[:, None, :], scores, jnp.float32(-1e30))
    newest = jnp.maximum(maxima, jnp.max(scores, axis=-1))
    weights = jnp.exp(scores - newest[..., None])
    if visible is not None:
        weights = jnp.where(visible[:, None, :], weights, jnp.float32(0.0))
    factor = jnp.exp(maxima - newest)
    totals = totals * factor + jnp.sum(weights, axis=-1)
    accumulated = accumulated * factor[..., None] + jnp.einsum(
        "qhk,khd->qhd",
        weights.astype(jnp.bfloat16),
        block_values,
        preferred_element_type=jnp.float32,
    )
    return (newest, totals, accumulated)


def on_device(hidden_in, norm_gain, w_qkv, w_out, prefix_kv, segment):
    row_count = hidden_in.shape[0]
    local_width = w_qkv.shape[2]
    head_count = local_width // HD
    gathered = lax.all_gather(hidden_in, "tp", axis=1, tiled=True)
    normed = layer_norm(gathered, norm_gain)
    projected = jnp.einsum("td,dce->tce", normed, w_qkv, preferred_element_type=jnp.float32)
    seg_row = segment[0]
    labels = jnp.arange(REQS, dtype=jnp.int32)
    onehot = (seg_row[:, None] == labels[None, :]).astype(jnp.int32)
    counts = jnp.sum(onehot, axis=0)
    all_counts = lax.all_gather(counts[None, :], "blk", axis=0, tiled=True)
    request_sizes = jnp.sum(all_counts, axis=0)
    request_ends = jnp.sum(
        jnp.where(labels[None, :] <= labels[:, None], request_sizes[None, :], 0), axis=1
    )
    request_starts = request_ends - request_sizes
    cycle_size = lax.axis_size("blk")
    cycle_place = lax.axis_index("blk")
    row_index = jnp.arange(row_count, dtype=jnp.int32)
    query_index = cycle_place * row_count + row_index
    within = query_index - jnp.sum(onehot * request_starts[None, :], axis=1)
    prefix_len = prefix_kv.shape[0] * lax.axis_size("grp") * cycle_size
    positions = within.astype(jnp.float32) + float(prefix_len)
    queries = rotary(projected[:, 0].reshape(row_count, head_count, HD), positions).astype(
        jnp.bfloat16
    )
    key_heads = rotary(projected[:, 1].reshape(row_count, head_count, HD), positions).astype(
        jnp.bfloat16
    )
    values = projected[:, 2].astype(jnp.bfloat16)
    keys_values = jnp.stack([key_heads.reshape(row_count, local_width), values], axis=1)
    score_scale = 1.0 / math.sqrt(HD)
    running = (
        jnp.full((row_count, head_count), -1e30, jnp.float32),
        jnp.zeros((row_count, head_count), jnp.float32),
        jnp.zeros((row_count, head_count, HD), jnp.float32),
    )
    running = attend_block(
        running,
        queries,
        lax.all_gather(prefix_kv, ("grp", "blk"), axis=0, tiled=True),
        None,
        score_scale,
    )
    block_kv = lax.all_gather(keys_values, "blk", axis=0, tiled=True)
    key_index = jnp.arange(block_kv.shape[0], dtype=jnp.int32)
    key_segment = jnp.sum((key_index[:, None] >= request_ends[None, :]).astype(jnp.int32), axis=1)
    visible = (
        (key_segment[None, :] == seg_row[:, None])
        & (key_index[None, :] <= query_index[:, None])
        & True
    )

    def take_block(kept):
        return attend_block(kept, queries, block_kv, visible, score_scale)

    def skip_block(kept):
        return kept

    running = lax.cond(jnp.any(visible), take_block, skip_block, running)
    maxima, totals, accumulated = running
    attention = (
        (accumulated / totals[..., None]).astype(jnp.bfloat16).reshape(row_count, local_width)
    )
    attended = lax.psum_scatter(
        jnp.dot(attention, w_out, preferred_element_type=jnp.float32).astype(jnp.bfloat16),
        "tp",
        scatter_dimension=0,
        tiled=True,
    )
    return (attended, keys_values)


LANES = 128
CHUNK = 512
OUT_CHUNK = 512
DELIVER = 2
MESH = pl.DeviceIdType.MESH


def head_pairs(block):
    wide = block.astype(jnp.float32)
    lane = lax.broadcasted_iota(jnp.int32, wide.shape, 1)
    first = jnp.where(lane < HD, wide, 0.0)
    second = jnp.where(lane < HD, 0.0, wide)
    return jnp.concatenate([first, second], axis=0).astype(jnp.bfloat16)


def attend_step(stacked, keys, values, mask, state):
    factor = math.log2(math.e) / math.sqrt(HD)
    scores = lax.dot_general(
        stacked, keys, (((1,), (1,)), ((), ())), preferred_element_type=jnp.float32
    )
    if mask is not None:
        rows = mask.shape[0]
        scores = jnp.concatenate(
            [
                jnp.where(mask, scores[:rows], jnp.float32(-1e30)),
                jnp.where(mask, scores[rows:], jnp.float32(-1e30)),
            ],
            axis=0,
        )
    top = jnp.max(scores, axis=1, keepdims=True)
    if state is not None:
        top = jnp.maximum(top, state[0])
    weights = jnp.exp2((scores - top) * factor)
    total = jnp.sum(weights, axis=1, keepdims=True)
    summed = jnp.dot(weights.astype(jnp.bfloat16), values, preferred_element_type=jnp.float32)
    if state is not None:
        shrink = jnp.exp2((state[0] - top) * factor)
        total = total + state[1] * shrink
        summed = summed + state[2] * shrink
    return top, total, summed


def block_kernel(
    n_blk,
    hid_ref,
    gain_ref,
    w_ref,
    wo_ref,
    pre_ref,
    seg_ref,
    inv_ref,
    out_ref,
    kv_ref,
    wbuf,
    wobuf,
    hid_other,
    normed,
    pre_out,
    pre_all,
    seg_out,
    seg_all,
    seg_flat,
    seg_col,
    send_buf,
    qkv,
    top_s,
    total_s,
    sum_s,
    obuf,
    attn_in,
    attn,
    low,
    part,
    part_other,
    w_sem,
    wo_sem,
    hid_sem,
    seg_send,
    seg_recv,
    pre_send,
    pre_recv,
    qkv_send,
    qkv_recv,
    o_send,
    o_recv,
    part_send,
    part_recv,
):
    g, b, t = lax.axis_index("grp"), lax.axis_index("blk"), lax.axis_index("tp")
    rows, half = hid_ref.shape
    model = 2 * half
    pre_rows = pre_ref.shape[0]
    n_z = n_blk // 2
    z, x = b // 2, b % 2
    partner = (g, b, 1 - t)
    across = (1 - g, b, t)

    def dest(n):
        flip = (n_z - 1) - n // 2
        z_high = (z // 2 + flip // 2) % 2
        z_low = (z % 2 + flip % 2) % 2
        return (z_high * 2 + z_low) * 2 + (x + 1 + n) % 2

    def lanes(block):
        return pl.ds(pl.multiple_of(block * LANES, LANES), LANES)

    def token_rows(block):
        return pl.ds(pl.multiple_of(block * rows, rows), rows)

    w_copies = []
    for n in range(n_blk):
        copy = pltpu.make_async_copy(
            w_ref.at[:, :, lanes(dest(n))],
            wbuf.at[n // 2, :, :, pl.ds((n % 2) * LANES, LANES)],
            w_sem.at[n],
        )
        copy.start()
        w_copies.append(copy)
    wo_copy = pltpu.make_async_copy(wo_ref, wobuf, wo_sem)
    wo_copy.start()

    barrier = pltpu.get_barrier_semaphore()
    pl.semaphore_signal(barrier, inc=1, device_id=partner, device_id_type=MESH)
    pl.semaphore_signal(barrier, inc=1, device_id=across, device_id_type=MESH)
    for k in range(1, n_blk):
        pl.semaphore_signal(
            barrier, inc=1, device_id=(g, (b + k) % n_blk, t), device_id_type=MESH
        )
    for d in range(n_blk):
        for c in range(2):
            pre_out[d, c] = pre_ref[:, c, d * LANES : (d + 1) * LANES]
    seg_out[...] = jnp.broadcast_to(seg_ref[...], seg_out.shape)
    pl.semaphore_wait(barrier, n_blk + 1)

    hid_copy = pltpu.make_async_remote_copy(
        hid_ref, hid_other, hid_sem.at[0], hid_sem.at[1], device_id=partner, device_id_type=MESH
    )
    hid_copy.start()

    def seg_copy(k, slot):
        return pltpu.make_async_remote_copy(
            seg_out,
            seg_all.at[slot],
            seg_send.at[k],
            seg_recv.at[slot],
            device_id=(g, (b + k) % n_blk, t),
            device_id_type=MESH,
        )

    for k in range(1, n_blk):
        seg_copy(k, b).start()

    def pre_slot(slot):
        return pre_all.at[:, pl.ds(pl.multiple_of(slot * pre_rows, pre_rows), pre_rows), :]

    def pre_copy(k, slot):
        peer_b = (b + k) % n_blk
        return pltpu.make_async_remote_copy(
            pre_out.at[peer_b],
            pre_slot(slot),
            pre_send.at[k],
            pre_recv.at[slot],
            device_id=(g, peer_b, t),
            device_id_type=MESH,
        )

    def forward_copy(k, slot):
        return pltpu.make_async_remote_copy(
            pre_slot(slot),
            pre_slot(slot),
            pre_send.at[n_blk + k],
            pre_recv.at[slot],
            device_id=across,
            device_id_type=MESH,
        )

    def slot_of(group, k):
        return group * n_blk + (b + k) % n_blk

    my_slot = slot_of(g, 0)
    for n in range(n_blk - 1):
        k = (dest(n) - b + n_blk) % n_blk
        pre_copy(k, my_slot).start()
    pre_all[:, pl.ds(pl.multiple_of(my_slot * pre_rows, pre_rows), pre_rows), :] = pre_out[b]
    forward_copy(0, my_slot).start()
    seg_all[b] = seg_out[...]

    for k in range(1, n_blk):
        seg_copy(k, (b + k) % n_blk).wait_recv()
    for c in range(n_blk):
        row = seg_all[c].astype(jnp.float32)
        seg_flat[:, c * rows : (c + 1) * rows] = row
        seg_col[c] = jnp.broadcast_to(row[:1], (rows, rows)).T
    own_seg = seg_col[b][:, :1]
    before = jnp.where(seg_flat[:1] < own_seg, 1.0, 0.0)
    start = jnp.sum(before, axis=1, keepdims=True)
    row_iota = lax.broadcasted_iota(jnp.int32, (rows, LANES), 0)
    prefix_len = float(2 * n_blk * pre_rows)
    position = (b * rows + row_iota).astype(jnp.float32) - start + prefix_len
    angles = position * inv_ref[:1]
    in_head = lax.broadcasted_iota(jnp.int32, (rows, LANES), 1) % HD
    rotated = HD // 4
    sine = jnp.sin(angles)
    cos_t = jnp.where(in_head < rotated, jnp.cos(angles), 1.0)
    low_t = jnp.where(in_head < rotated // 2, -sine, 0.0)
    high_t = jnp.where((in_head >= rotated // 2) & (in_head < rotated), sine, 0.0)

    hid_copy.wait()
    mine = hid_ref[...].astype(jnp.float32)
    other = hid_other[...].astype(jnp.float32)
    mean = (
        jnp.sum(mine, axis=1, keepdims=True) + jnp.sum(other, axis=1, keepdims=True)
    ) * (1.0 / model)
    mine = mine - mean
    other = other - mean
    variance = (
        jnp.sum(mine * mine, axis=1, keepdims=True)
        + jnp.sum(other * other, axis=1, keepdims=True)
    ) * (1.0 / model)
    scale = lax.rsqrt(variance + 1e-05)
    mine_cols = pl.ds(pl.multiple_of(t * half, half), half)
    other_cols = pl.ds(pl.multiple_of((1 - t) * half, half), half)
    normed[:, mine_cols] = (mine * scale * gain_ref[:, mine_cols]).astype(jnp.bfloat16)
    normed[:, other_cols] = (other * scale * gain_ref[:, other_cols]).astype(jnp.bfloat16)

    def qkv_copy(n, slot):
        return pltpu.make_async_remote_copy(
            send_buf.at[n],
            qkv.at[:, token_rows(slot), :],
            qkv_send.at[n],
            qkv_recv.at[slot],
            device_id=(g, dest(n), t),
            device_id_type=MESH,
        )

    for i in range(n_z):
        w_copies[2 * i].wait()
        w_copies[2 * i + 1].wait()
        for c in range(3):
            product = jnp.dot(normed[...], wbuf[i, c], preferred_element_type=jnp.float32)
            for h in range(2):
                n = 2 * i + h
                tile = product[:, h * LANES : (h + 1) * LANES]
                if c < 2:
                    tile = (
                        tile * cos_t
                        + pltpu.roll(tile, LANES - rotated // 2, 1) * low_t
                        + pltpu.roll(tile, rotated // 2, 1) * high_t
                    )
                tile = tile.astype(jnp.bfloat16)
                send_buf[n, c] = tile
                if c > 0:
                    kv_ref[:, c - 1, lanes(dest(n))] = tile
        for h in range(2):
            n = 2 * i + h
            if n < n_blk - 1:
                qkv_copy(n, b).start()
    qkv[:, token_rows(b), :] = send_buf[n_blk - 1]

    for k in range(1, n_blk):
        pre_copy(k, slot_of(g, k)).wait_recv()
        forward_copy(k, slot_of(g, k)).start()
    for k in range(n_blk):
        forward_copy(k, slot_of(1 - g, k)).wait_recv()

    def o_copy(n, to, slot):
        return pltpu.make_async_remote_copy(
            obuf.at[n],
            attn_in.at[slot],
            o_send.at[n],
            o_recv.at[slot],
            device_id=(g, to, t),
            device_id_type=MESH,
        )

    near = n_blk // 2
    own_half = z // 2

    def queries(block):
        return head_pairs(qkv[0, token_rows(block), :])

    def prefix_step(block):
        return attend_step(queries(block), pre_all[0], pre_all[1], None, None)

    def half_step(block, c, state):
        q_seg = seg_col[block][:, :1]
        q_index = block * rows + lax.broadcasted_iota(jnp.int32, (rows, CHUNK), 0)
        k_index = c * CHUNK + lax.broadcasted_iota(jnp.int32, (rows, CHUNK), 1)
        keys = slice(c * CHUNK, (c + 1) * CHUNK)
        mask = (seg_flat[:1, keys] == q_seg) & (k_index <= q_index)
        return attend_step(queries(block), qkv[1, keys, :], qkv[2, keys, :], mask, state)

    def keep(block, state):
        top_s[block], total_s[block], sum_s[block] = state

    def kept(block):
        return top_s[block], total_s[block], sum_s[block]

    def finish(numbers, states):
        lane = lax.broadcasted_iota(jnp.int32, (rows, LANES), 1)
        for n, (_, total, summed) in zip(numbers, states):
            result = summed / total
            obuf[n] = jnp.where(lane < HD, result[:rows], result[rows:]).astype(jnp.bfloat16)
        for n in numbers:

            @pl.when(n < n_blk - 1)
            def _():
                o_copy(n, dest(n), b).start()

    def pair(first, m):
        return first + 2 * m, first + 2 * m + 1

    for n in range(near, n_blk - 1):
        qkv_copy(n, dest(n)).wait_recv()

    @pl.when(own_half == 0)
    def _():
        @pl.loop(0, near // 2)
        def _(m):
            numbers = pair(near, m)
            finish(numbers, [half_step(dest(n), 0, prefix_step(dest(n))) for n in numbers])

        @pl.loop(0, near)
        def _(n):
            qkv_copy(n, dest(n)).wait_recv()
            keep(dest(n), half_step(dest(n), 0, prefix_step(dest(n))))

        @pl.loop(0, near // 2)
        def _(m):
            numbers = pair(0, m)
            finish(numbers, [half_step(dest(n), 1, kept(dest(n))) for n in numbers])

    @pl.when(own_half == 1)
    def _():
        @pl.loop(0, near // 2)
        def _(m):
            numbers = pair(near, m)
            states = [half_step(dest(n), 1, prefix_step(dest(n))) for n in numbers]
            for n, state in zip(numbers, states):
                keep(dest(n), state)

        @pl.loop(0, near)
        def _(n):
            qkv_copy(n, dest(n)).wait_recv()
            keep(dest(n), prefix_step(dest(n)))

        @pl.loop(0, near)
        def _(m):
            numbers = pair(0, m)
            finish(numbers, [half_step(dest(n), 0, kept(dest(n))) for n in numbers])

    attn_in[b] = obuf[n_blk - 1]
    wo_copy.wait()

    def arrived(half):
        for c in range(half * near, (half + 1) * near):

            @pl.when(c != b)
            def _():
                o_copy(0, dest(0), c).wait_recv()

        return jnp.concatenate([attn_in[half * near + c] for c in range(near)], axis=1)

    depth = near * LANES
    attn_low = arrived(0)
    low[...] = jnp.dot(attn_low, wobuf[:depth, :], preferred_element_type=jnp.float32)
    attn[...] = arrived(1)

    share = rows // 2
    n_out = model // OUT_CHUNK
    mine_rows = pl.ds(pl.multiple_of(t * share, share), share)
    other_rows = pl.ds(pl.multiple_of((1 - t) * share, share), share)
    part_copies = []
    for j in range(n_out):
        cols = slice(j * OUT_CHUNK, (j + 1) * OUT_CHUNK)
        product = low[:, cols] + jnp.dot(
            attn[...], wobuf[depth:, cols], preferred_element_type=jnp.float32
        )
        part[j] = product.astype(jnp.bfloat16)
        copy = pltpu.make_async_remote_copy(
            part.at[j, other_rows, :],
            part_other.at[j],
            part_send.at[j],
            part_recv.at[j],
            device_id=partner,
            device_id_type=MESH,
        )
        copy.start()
        part_copies.append(copy)
    for j in range(n_out):
        part_copies[j].wait_recv()
        out_ref[:, j * OUT_CHUNK : (j + 1) * OUT_CHUNK] = (
            part[j, mine_rows, :].astype(jnp.float32) + part_other[j].astype(jnp.float32)
        ).astype(jnp.bfloat16)

    for copy in part_copies:
        copy.wait_send()
    for n in range(n_blk - 1):
        qkv_copy(n, b).wait_send()
        o_copy(n, dest(n), b).wait_send()
    for k in range(1, n_blk):
        seg_copy(k, b).wait_send()
    for k in range(1, n_blk):
        pre_copy(k, my_slot).wait_send()
    for k in range(n_blk):
        forward_copy(k, slot_of(g, k)).wait_send()


def on_device_heads(hidden_in, norm_gain, w_qkv, w_out, prefix_kv, segment):
    rows, half = hidden_in.shape
    model = 2 * half
    width = w_qkv.shape[2]
    n_blk = width // LANES
    tokens = n_blk * rows
    pre_rows = prefix_kv.shape[0]
    rotated = HD // 4
    inverse = 10000.0 ** (-(np.arange(rotated // 2) * 2.0) / rotated)
    inverse = jnp.asarray(np.tile(inverse, (8, LANES // (rotated // 2))), jnp.float32)
    vmem = pl.BlockSpec(memory_space=pltpu.VMEM)
    hbm = pl.BlockSpec(memory_space=pl.ANY)
    bf16, f32 = jnp.bfloat16, jnp.float32
    dma = pltpu.SemaphoreType.DMA
    n_out = model // OUT_CHUNK

    def kernel(*refs):
        block_kernel(n_blk, *refs)

    attended, stacked = pl.pallas_call(
        kernel,
        name="attention_block",
        out_shape=(
            pltpu.VMEM((rows // 2, model), bf16),
            pltpu.VMEM((rows, 2, width), bf16),
        ),
        in_specs=[vmem, vmem, hbm, hbm, vmem, vmem, vmem],
        out_specs=(vmem, vmem),
        scratch_shapes=[
            pltpu.VMEM((n_blk // 2, 3, model, 2 * LANES), bf16),
            pltpu.VMEM((width, model), bf16),
            pltpu.VMEM((rows, half), bf16),
            pltpu.VMEM((rows, model), bf16),
            pltpu.VMEM((n_blk, 2, pre_rows, LANES), bf16),
            pltpu.VMEM((2, 2 * n_blk * pre_rows, LANES), bf16),
            pltpu.VMEM((8, rows), jnp.int32),
            pltpu.VMEM((n_blk, 8, rows), jnp.int32),
            pltpu.VMEM((8, tokens), f32),
            pltpu.VMEM((n_blk, rows, rows), f32),
            pltpu.VMEM((n_blk, 3, rows, LANES), bf16),
            pltpu.VMEM((3, tokens, LANES), bf16),
            pltpu.VMEM((n_blk, 2 * rows, 1), f32),
            pltpu.VMEM((n_blk, 2 * rows, 1), f32),
            pltpu.VMEM((n_blk, 2 * rows, LANES), f32),
            pltpu.VMEM((n_blk, rows, LANES), bf16),
            pltpu.VMEM((n_blk, rows, LANES), bf16),
            pltpu.VMEM((rows, width // 2), bf16),
            pltpu.VMEM((rows, model), f32),
            pltpu.VMEM((n_out, rows, OUT_CHUNK), bf16),
            pltpu.VMEM((n_out, rows // 2, OUT_CHUNK), bf16),
            dma((n_blk,)),
            dma,
            dma((2,)),
            dma((n_blk,)),
            dma((n_blk,)),
            dma((2 * n_blk,)),
            dma((2 * n_blk,)),
            dma((n_blk,)),
            dma((n_blk,)),
            dma((n_blk,)),
            dma((n_blk,)),
            dma((n_out,)),
            dma((n_out,)),
        ],
        compiler_params=pltpu.CompilerParams(
            collective_id=0, has_side_effects=True, vmem_limit_bytes=56 * 1024 * 1024
        ),
    )(
        hidden_in,
        norm_gain[None, :],
        jnp.transpose(w_qkv, (1, 0, 2)),
        w_out,
        prefix_kv,
        segment,
        inverse,
    )
    return deliver(attended, stacked)


def deliver_kernel(attended_ref, stacked_ref, out_ref, kv_ref, sem):
    copies = []
    for n, (source, target) in enumerate(((stacked_ref, kv_ref), (attended_ref, out_ref))):
        share = source.shape[0] // DELIVER
        for i in range(DELIVER):
            part = pl.ds(i * share, share)
            copy = pltpu.make_async_copy(source.at[part], target.at[part], sem.at[n, i])
            copy.start()
            copies.append(copy)
    for copy in copies:
        copy.wait()


def deliver(attended, stacked):
    anywhere = pl.BlockSpec(memory_space=pl.ANY)
    inside = pl.BlockSpec(memory_space=pltpu.VMEM)
    return pl.pallas_call(
        deliver_kernel,
        name="deliver",
        out_shape=(
            jax.ShapeDtypeStruct(attended.shape, attended.dtype),
            jax.ShapeDtypeStruct(stacked.shape, stacked.dtype),
        ),
        in_specs=[inside, inside],
        out_specs=(anywhere, anywhere),
        scratch_shapes=[pltpu.SemaphoreType.DMA((2, DELIVER))],
    )(
        pltpu.with_memory_space_constraint(attended, pltpu.VMEM),
        pltpu.with_memory_space_constraint(stacked, pltpu.VMEM),
    )


def by_heads(hidden_in, norm_gain, w_qkv, w_out, prefix_kv, segment):
    rows, half = hidden_in.shape
    n_blk = lax.axis_size("blk")
    fits = (
        lax.axis_size("grp") == 2
        and lax.axis_size("tp") == 2
        and n_blk == 8
        and w_qkv.shape[2] == n_blk * LANES
        and rows == LANES
        and n_blk * rows == 2 * CHUNK
        and half % OUT_CHUNK == 0
        and prefix_kv.shape[0] % 16 == 0
    )
    form = on_device_heads if fits else on_device
    return form(hidden_in, norm_gain, w_qkv, w_out, prefix_kv, segment)


def solution(mesh):
    placed = (
        P(("grp", "blk"), "tp"),
        P(),
        P(None, None, "tp"),
        P("tp", None),
        P(("grp", "blk"), None, "tp"),
        P("grp", "blk"),
    )
    return jax.shard_map(
        by_heads,
        mesh=mesh,
        in_specs=placed,
        out_specs=(P(("grp", "blk", "tp"), None), P(("grp", "blk"), None, "tp")),
        check_vma=False,
    )
```

```python
import math

import jax
import jax.numpy as jnp
import numpy as np
from jax import lax
from jax.experimental import pallas as pl
from jax.experimental.pallas import tpu as pltpu
from jax.sharding import PartitionSpec as P

HD = 64
REQS = 8


def layer_norm(matrix_rows, norm_gain):
    values_f = matrix_rows.astype(jnp.float32)
    row_mean = jnp.mean(values_f, axis=-1, keepdims=True)
    centered = values_f - row_mean
    variance = jnp.mean(centered * centered, axis=-1, keepdims=True)
    return (centered * lax.rsqrt(variance + 1e-05) * norm_gain).astype(jnp.bfloat16)


def rotary(heads_f, positions):
    head_size = heads_f.shape[-1]
    rotated = head_size // 4
    half_rot = rotated // 2
    inverse = 10000.0 ** (-(jnp.arange(half_rot, dtype=jnp.float32) * 2.0) / rotated)
    angles = positions[:, None] * inverse[None, :]
    cos_table = jnp.cos(angles)[:, None, :]
    sine_table = jnp.sin(angles)[:, None, :]
    first_half = heads_f[..., :half_rot]
    second_half = heads_f[..., half_rot:rotated]
    return jnp.concatenate(
        [
            first_half * cos_table - second_half * sine_table,
            second_half * cos_table + first_half * sine_table,
            heads_f[..., rotated:],
        ],
        axis=-1,
    )


def attend_block(carried, queries, block_kv, visible, score_scale):
    maxima, totals, accumulated = carried
    key_count = block_kv.shape[0]
    head_count = queries.shape[1]
    block_keys = block_kv[:, 0].reshape(key_count, head_count, HD)
    block_values = block_kv[:, 1].reshape(key_count, head_count, HD)
    scores = (
        jnp.einsum("qhd,khd->qhk", queries, block_keys, preferred_element_type=jnp.float32)
        * score_scale
    )
    if visible is not None:
        scores = jnp.where(visible[:, None, :], scores, jnp.float32(-1e30))
    newest = jnp.maximum(maxima, jnp.max(scores, axis=-1))
    weights = jnp.exp(scores - newest[..., None])
    if visible is not None:
        weights = jnp.where(visible[:, None, :], weights, jnp.float32(0.0))
    factor = jnp.exp(maxima - newest)
    totals = totals * factor + jnp.sum(weights, axis=-1)
    accumulated = accumulated * factor[..., None] + jnp.einsum(
        "qhk,khd->qhd",
        weights.astype(jnp.bfloat16),
        block_values,
        preferred_element_type=jnp.float32,
    )
    return (newest, totals, accumulated)


def on_device(hidden_in, norm_gain, w_qkv, w_out, prefix_kv, segment):
    row_count = hidden_in.shape[0]
    local_width = w_qkv.shape[2]
    head_count = local_width // HD
    gathered = lax.all_gather(hidden_in, "tp", axis=1, tiled=True)
    normed = layer_norm(gathered, norm_gain)
    projected = jnp.einsum("td,dce->tce", normed, w_qkv, preferred_element_type=jnp.float32)
    seg_row = segment[0]
    labels = jnp.arange(REQS, dtype=jnp.int32)
    onehot = (seg_row[:, None] == labels[None, :]).astype(jnp.int32)
    counts = jnp.sum(onehot, axis=0)
    all_counts = lax.all_gather(counts[None, :], "blk", axis=0, tiled=True)
    request_sizes = jnp.sum(all_counts, axis=0)
    request_ends = jnp.sum(
        jnp.where(labels[None, :] <= labels[:, None], request_sizes[None, :], 0), axis=1
    )
    request_starts = request_ends - request_sizes
    cycle_size = lax.axis_size("blk")
    cycle_place = lax.axis_index("blk")
    row_index = jnp.arange(row_count, dtype=jnp.int32)
    query_index = cycle_place * row_count + row_index
    within = query_index - jnp.sum(onehot * request_starts[None, :], axis=1)
    prefix_len = prefix_kv.shape[0] * lax.axis_size("grp") * cycle_size
    positions = within.astype(jnp.float32) + float(prefix_len)
    queries = rotary(projected[:, 0].reshape(row_count, head_count, HD), positions).astype(
        jnp.bfloat16
    )
    key_heads = rotary(projected[:, 1].reshape(row_count, head_count, HD), positions).astype(
        jnp.bfloat16
    )
    values = projected[:, 2].astype(jnp.bfloat16)
    keys_values = jnp.stack([key_heads.reshape(row_count, local_width), values], axis=1)
    score_scale = 1.0 / math.sqrt(HD)
    running = (
        jnp.full((row_count, head_count), -1e30, jnp.float32),
        jnp.zeros((row_count, head_count), jnp.float32),
        jnp.zeros((row_count, head_count, HD), jnp.float32),
    )
    running = attend_block(
        running,
        queries,
        lax.all_gather(prefix_kv, ("grp", "blk"), axis=0, tiled=True),
        None,
        score_scale,
    )
    block_kv = lax.all_gather(keys_values, "blk", axis=0, tiled=True)
    key_index = jnp.arange(block_kv.shape[0], dtype=jnp.int32)
    key_segment = jnp.sum((key_index[:, None] >= request_ends[None, :]).astype(jnp.int32), axis=1)
    visible = (
        (key_segment[None, :] == seg_row[:, None])
        & (key_index[None, :] <= query_index[:, None])
        & True
    )

    def take_block(kept):
        return attend_block(kept, queries, block_kv, visible, score_scale)

    def skip_block(kept):
        return kept

    running = lax.cond(jnp.any(visible), take_block, skip_block, running)
    maxima, totals, accumulated = running
    attention = (
        (accumulated / totals[..., None]).astype(jnp.bfloat16).reshape(row_count, local_width)
    )
    attended = lax.psum_scatter(
        jnp.dot(attention, w_out, preferred_element_type=jnp.float32).astype(jnp.bfloat16),
        "tp",
        scatter_dimension=0,
        tiled=True,
    )
    return (attended, keys_values)


LANES = 128
OUT_CHUNK = 512
DELIVER = 2
MESH = pl.DeviceIdType.MESH


def head_pairs(block):
    wide = block.astype(jnp.float32)
    lane = lax.broadcasted_iota(jnp.int32, wide.shape, 1)
    first = jnp.where(lane < HD, wide, 0.0)
    second = jnp.where(lane < HD, 0.0, wide)
    return jnp.concatenate([first, second], axis=0).astype(jnp.bfloat16)


def attend_step(stacked, keys, values, mask, state):
    factor = math.log2(math.e) / math.sqrt(HD)
    scores = lax.dot_general(
        stacked, keys, (((1,), (1,)), ((), ())), preferred_element_type=jnp.float32
    )
    if mask is not None:
        rows = mask.shape[0]
        scores = jnp.concatenate(
            [
                jnp.where(mask, scores[:rows], jnp.float32(-1e30)),
                jnp.where(mask, scores[rows:], jnp.float32(-1e30)),
            ],
            axis=0,
        )
    top = jnp.max(scores, axis=1, keepdims=True)
    if state is not None:
        top = jnp.maximum(top, state[0])
    weights = jnp.exp2((scores - top) * factor)
    total = jnp.sum(weights, axis=1, keepdims=True)
    summed = jnp.dot(weights.astype(jnp.bfloat16), values, preferred_element_type=jnp.float32)
    if state is not None:
        shrink = jnp.exp2((state[0] - top) * factor)
        total = total + state[1] * shrink
        summed = summed + state[2] * shrink
    return top, total, summed


def block_kernel(
    n_blk,
    hid_ref,
    gain_ref,
    w_ref,
    wo_ref,
    pre_ref,
    seg_ref,
    inv_ref,
    out_ref,
    kv_ref,
    wbuf,
    wobuf,
    hid_mine,
    hid_other,
    pre_mine,
    normed,
    pre_out,
    pre_all,
    seg_out,
    seg_all,
    seg_flat,
    seg_col,
    send_buf,
    qkv,
    top_s,
    total_s,
    sum_s,
    obuf,
    attn_in,
    attn,
    low,
    part,
    part_other,
    in_sem,
    w_sem,
    wo_sem,
    hid_sem,
    seg_send,
    seg_recv,
    pre_send,
    pre_recv,
    qkv_send,
    qkv_recv,
    o_send,
    o_recv,
    part_send,
    part_recv,
):
    g, b, t = lax.axis_index("grp"), lax.axis_index("blk"), lax.axis_index("tp")
    rows, half = hid_mine.shape
    model = 2 * half
    pre_rows = pre_mine.shape[0]
    n_z = n_blk // 2
    near = n_blk // 2
    z, x = b // 2, b % 2
    side = z // 2
    near_base, far_base = side * near, (1 - side) * near
    partner = (g, b, 1 - t)
    across = (1 - g, b, t)

    def dest_z(i):
        flip = n_z - 1 - i
        return (z // 2 + flip // 2) % 2 * 2 + (z % 2 + flip % 2) % 2

    def dest(n):
        return dest_z(n // 2) * 2 + (x + 1 + n) % 2

    def lanes(block):
        return pl.ds(pl.multiple_of(block * LANES, LANES), LANES)

    def token_rows(block):
        return pl.ds(pl.multiple_of(block * rows, rows), rows)

    barrier = pltpu.get_barrier_semaphore()
    pl.semaphore_signal(barrier, inc=1, device_id=partner, device_id_type=MESH)
    pl.semaphore_signal(barrier, inc=1, device_id=across, device_id_type=MESH)
    for n in range(n_blk - 1):
        pl.semaphore_signal(barrier, inc=1, device_id=(g, dest(n), t), device_id_type=MESH)

    pre_load = pltpu.make_async_copy(pre_ref, pre_mine, in_sem.at[0])
    pre_load.start()
    hid_load = pltpu.make_async_copy(hid_ref, hid_mine, in_sem.at[1])
    hid_load.start()
    pre_load.wait()
    hid_load.wait()

    def w_cols(i):
        return pl.ds(pl.multiple_of(dest_z(i) * 2 * LANES, 2 * LANES), 2 * LANES)

    def w_load(c, i):
        return pltpu.make_async_copy(
            w_ref.at[c, :, w_cols(i)], wbuf.at[i, c], w_sem.at[c * n_z + i]
        )

    for c in (2, 0, 1):
        for i in range(n_z):
            w_load(c, i).start()
    wo_copy = pltpu.make_async_copy(wo_ref, wobuf, wo_sem)
    wo_copy.start()

    seg_out[...] = jnp.broadcast_to(seg_ref[...], seg_out.shape)
    for d in range(n_blk):
        for c in range(2):
            pre_out[d, c] = pre_mine[:, c, d * LANES : (d + 1) * LANES]
    pl.semaphore_wait(barrier, n_blk + 1)

    hid_copy = pltpu.make_async_remote_copy(
        hid_mine, hid_other, hid_sem.at[0], hid_sem.at[1], device_id=partner, device_id_type=MESH
    )
    hid_copy.start()

    def seg_copy(n, slot):
        return pltpu.make_async_remote_copy(
            seg_out,
            seg_all.at[slot],
            seg_send.at[n],
            seg_recv.at[slot],
            device_id=(g, dest(n), t),
            device_id_type=MESH,
        )

    for n in range(n_blk - 1):
        seg_copy(n, b).start()

    def pre_slot(slot):
        return pre_all.at[:, pl.ds(pl.multiple_of(slot * pre_rows, pre_rows), pre_rows), :]

    def pre_copy(n, slot):
        return pltpu.make_async_remote_copy(
            pre_out.at[dest(n)],
            pre_slot(slot),
            pre_send.at[n],
            pre_recv.at[slot],
            device_id=(g, dest(n), t),
            device_id_type=MESH,
        )

    def forward_copy(n, slot):
        return pltpu.make_async_remote_copy(
            pre_slot(slot),
            pre_slot(slot),
            pre_send.at[n_blk + n],
            pre_recv.at[slot],
            device_id=across,
            device_id_type=MESH,
        )

    my_slot = g * n_blk + b
    for n in range(n_blk - 1):
        pre_copy(n, my_slot).start()
    pre_all[:, pl.ds(pl.multiple_of(my_slot * pre_rows, pre_rows), pre_rows), :] = pre_out[b]
    forward_copy(n_blk - 1, my_slot).start()
    seg_all[b] = seg_out[...]

    def pass_on(numbers):
        for n in numbers:
            slot = g * n_blk + dest(n)
            pre_copy(n, slot).wait_recv()
            forward_copy(n, slot).start()

    mine = hid_mine[...].astype(jnp.float32)
    mine_sum = jnp.sum(mine, axis=1, keepdims=True)
    hid_copy.wait()
    other = hid_other[...].astype(jnp.float32)
    mean = (mine_sum + jnp.sum(other, axis=1, keepdims=True)) * (1.0 / model)
    mine = mine - mean
    other = other - mean
    variance = (
        jnp.sum(mine * mine, axis=1, keepdims=True)
        + jnp.sum(other * other, axis=1, keepdims=True)
    ) * (1.0 / model)
    scale = lax.rsqrt(variance + 1e-05)
    mine_cols = pl.ds(pl.multiple_of(t * half, half), half)
    other_cols = pl.ds(pl.multiple_of((1 - t) * half, half), half)
    normed[:, mine_cols] = (mine * scale * gain_ref[:, mine_cols]).astype(jnp.bfloat16)
    normed[:, other_cols] = (other * scale * gain_ref[:, other_cols]).astype(jnp.bfloat16)

    def qkv_copy(c, n, slot):
        return pltpu.make_async_remote_copy(
            send_buf.at[n, c],
            qkv.at[c, token_rows(slot), :],
            qkv_send.at[c * n_blk + n],
            qkv_recv.at[c * n_blk + slot],
            device_id=(g, dest(n), t),
            device_id_type=MESH,
        )

    def start_others(c, i):
        for n in (2 * i, 2 * i + 1):
            if n < n_blk - 1:
                qkv_copy(c, n, b).start()

    for i in range(n_z):
        w_load(2, i).wait()
        product = jnp.dot(normed[...], wbuf[i, 2], preferred_element_type=jnp.float32)
        for h in range(2):
            tile = product[:, h * LANES : (h + 1) * LANES].astype(jnp.bfloat16)
            send_buf[2 * i + (x + 1 + h) % 2, 2] = tile
            kv_ref[:, 1, lanes(dest_z(i) * 2 + h)] = tile
        start_others(2, i)

    for n in range(n_blk - 1):
        seg_copy(n, dest(n)).wait_recv()
    for c in range(n_blk):
        row = seg_all[c].astype(jnp.float32)
        seg_flat[:, c * rows : (c + 1) * rows] = row
        seg_col[c] = jnp.broadcast_to(row[:1], (rows, rows)).T
    own_seg = seg_col[b][:, :1]
    before = jnp.where(seg_flat[:1] < own_seg, 1.0, 0.0)
    start = jnp.sum(before, axis=1, keepdims=True)
    row_iota = lax.broadcasted_iota(jnp.int32, (rows, LANES), 0)
    prefix_len = float(2 * n_blk * pre_rows)
    position = (b * rows + row_iota).astype(jnp.float32) - start + prefix_len
    angles = position * inv_ref[:1]
    in_head = lax.broadcasted_iota(jnp.int32, (rows, LANES), 1) % HD
    rotated = HD // 4
    sine = jnp.sin(angles)
    cos_t = jnp.where(in_head < rotated, jnp.cos(angles), 1.0)
    low_t = jnp.where(in_head < rotated // 2, -sine, 0.0)
    high_t = jnp.where((in_head >= rotated // 2) & (in_head < rotated), sine, 0.0)


    for m in range(2 * n_z):
        c, i = m // n_z, m % n_z
        w_load(c, i).wait()
        product = jnp.dot(normed[...], wbuf[i, c], preferred_element_type=jnp.float32)
        for h in range(2):
            tile = product[:, h * LANES : (h + 1) * LANES]
            tile = (
                tile * cos_t
                + pltpu.roll(tile, LANES - rotated // 2, 1) * low_t
                + pltpu.roll(tile, rotated // 2, 1) * high_t
            ).astype(jnp.bfloat16)
            send_buf[2 * i + (x + 1 + h) % 2, c] = tile
            if c == 1:
                kv_ref[:, 0, lanes(dest_z(i) * 2 + h)] = tile
        start_others(c, i)

    qkv[:, token_rows(b), :] = send_buf[n_blk - 1]
    pass_on((6, 5, 4, 3, 2, 1, 0))

    for c in range(n_blk):
        forward_copy(c, (1 - g) * n_blk + c).wait_recv()

    split = near * rows

    def o_copy(block, slot):
        return pltpu.make_async_remote_copy(
            obuf.at[block],
            attn_in.at[slot],
            o_send.at[block],
            o_recv.at[slot],
            device_id=(g, block, t),
            device_id_type=MESH,
        )

    def arrive(c, block):
        qkv_copy(c, 0, block).wait_recv()

    def queries(block):
        return head_pairs(qkv[0, token_rows(block), :])

    def prefix_step(block):
        return attend_step(queries(block), pre_all[0], pre_all[1], None, None)

    def half_step(block, c, state):
        q_seg = seg_col[block][:, :1]
        q_index = block * rows + lax.broadcasted_iota(jnp.int32, (rows, split), 0)
        k_index = c * split + lax.broadcasted_iota(jnp.int32, (rows, split), 1)
        keys = pl.ds(pl.multiple_of(c * split, split), split)
        mask = (seg_flat[pl.ds(0, 1), keys] == q_seg) & (k_index <= q_index)
        return attend_step(queries(block), qkv[1, keys, :], qkv[2, keys, :], mask, state)

    def keep(block, state):
        top_s[block], total_s[block], sum_s[block] = state

    def kept(block):
        return top_s[block], total_s[block], sum_s[block]

    def finish(blocks, states):
        lane = lax.broadcasted_iota(jnp.int32, (rows, LANES), 1)
        for block, (_, total, summed) in zip(blocks, states):
            result = summed / total
            obuf[block] = jnp.where(lane < HD, result[:rows], result[rows:]).astype(jnp.bfloat16)
        for block in blocks:

            @pl.when(block != b)
            def _():
                o_copy(block, b).start()

    for n in range(near, n_blk - 1):
        for c in range(3):
            arrive(c, dest(n))

    @pl.loop(0, near // 2)
    def _(m):
        blocks = (near_base + 2 * m, near_base + 2 * m + 1)
        states = [half_step(c, side, prefix_step(c)) for c in blocks]

        @pl.when(side == 0)
        def _():
            finish(blocks, states)

        @pl.when(side == 1)
        def _():
            for c, state in zip(blocks, states):
                keep(c, state)

    @pl.loop(0, near // 2)
    def _(m):
        blocks = (far_base + 2 * m, far_base + 2 * m + 1)
        for c in blocks:
            arrive(0, c)
        for c, state in zip(blocks, [prefix_step(c) for c in blocks]):
            keep(c, state)

        @pl.when(side == 0)
        def _():
            for c, state in zip(blocks, [half_step(c, 0, kept(c)) for c in blocks]):
                keep(c, state)

    for m in range(near):
        arrive(2, far_base + m)
        arrive(1, far_base + m)

    @pl.loop(0, (1 + side) * (near // 2))
    def _(m):
        first = (far_base + 2 * m) % n_blk
        blocks = (first, first + 1)
        finish(blocks, [half_step(c, 1 - side, kept(c)) for c in blocks])

    attn_in[b] = obuf[b]
    wo_copy.wait()

    def arrived(first, count):
        for m in range(count):

            @pl.when(first + m != b)
            def _():
                o_copy(0, first + m).wait_recv()

        return jnp.concatenate([attn_in[first + m] for m in range(count)], axis=1)

    def wo_rows(first, count):
        return pl.ds(pl.multiple_of(first * LANES, count * LANES), count * LANES)

    n_out = model // OUT_CHUNK

    def columns(j):
        return pl.ds(pl.multiple_of(j * OUT_CHUNK, OUT_CHUNK), OUT_CHUNK)

    near_rows, far_rows = wo_rows(near_base, near), wo_rows(far_base, near)
    attn[...] = arrived(near_base, near)

    @pl.loop(0, n_out)
    def _(j):
        low[:, columns(j)] = jnp.dot(
            attn[...], wobuf[near_rows, columns(j)], preferred_element_type=jnp.float32
        )

    attn[...] = arrived(far_base, near)

    share = rows // 2
    mine_rows = pl.ds(pl.multiple_of(t * share, share), share)
    other_rows = pl.ds(pl.multiple_of((1 - t) * share, share), share)

    def part_copy(j):
        return pltpu.make_async_remote_copy(
            part.at[j, other_rows, :],
            part_other.at[j],
            part_send.at[j],
            part_recv.at[j],
            device_id=partner,
            device_id_type=MESH,
        )

    @pl.loop(0, n_out)
    def _(j):
        product = low[:, columns(j)] + jnp.dot(
            attn[...], wobuf[far_rows, columns(j)], preferred_element_type=jnp.float32
        )
        part[j] = product.astype(jnp.bfloat16)
        part_copy(j).start()

    for j in range(n_out):
        part_copy(j).wait_recv()
        out_ref[:, j * OUT_CHUNK : (j + 1) * OUT_CHUNK] = (
            part[j, mine_rows, :].astype(jnp.float32) + part_other[j].astype(jnp.float32)
        ).astype(jnp.bfloat16)

    for j in range(n_out):
        part_copy(j).wait_send()
    for n in range(n_blk):

        if n < n_blk - 1:
            for c in range(3):
                qkv_copy(c, n, b).wait_send()
            o_copy(dest(n), b).wait_send()
        forward_copy(n, my_slot).wait_send()
    for n in range(n_blk - 1):
        seg_copy(n, b).wait_send()
        pre_copy(n, my_slot).wait_send()


def on_device_heads(hidden_in, norm_gain, w_qkv, w_out, prefix_kv, segment):
    rows, half = hidden_in.shape
    model = 2 * half
    width = w_qkv.shape[2]
    n_blk = width // LANES
    tokens = n_blk * rows
    pre_rows = prefix_kv.shape[0]
    rotated = HD // 4
    inverse = 10000.0 ** (-(np.arange(rotated // 2) * 2.0) / rotated)
    inverse = jnp.asarray(np.tile(inverse, (8, LANES // (rotated // 2))), jnp.float32)
    vmem = pl.BlockSpec(memory_space=pltpu.VMEM)
    hbm = pl.BlockSpec(memory_space=pl.ANY)
    bf16, f32 = jnp.bfloat16, jnp.float32
    dma = pltpu.SemaphoreType.DMA
    n_out = model // OUT_CHUNK

    def kernel(*refs):
        block_kernel(n_blk, *refs)

    attended, stacked = pl.pallas_call(
        kernel,
        name="attention_block",
        out_shape=(
            pltpu.VMEM((rows // 2, model), bf16),
            pltpu.VMEM((rows, 2, width), bf16),
        ),
        in_specs=[hbm, vmem, hbm, hbm, hbm, vmem, vmem],
        out_specs=(vmem, vmem),
        scratch_shapes=[
            pltpu.VMEM((n_blk // 2, 3, model, 2 * LANES), bf16),
            pltpu.VMEM((width, model), bf16),
            pltpu.VMEM((rows, half), bf16),
            pltpu.VMEM((rows, half), bf16),
            pltpu.VMEM((pre_rows, 2, width), bf16),
            pltpu.VMEM((rows, model), bf16),
            pltpu.VMEM((n_blk, 2, pre_rows, LANES), bf16),
            pltpu.VMEM((2, 2 * n_blk * pre_rows, LANES), bf16),
            pltpu.VMEM((8, rows), jnp.int32),
            pltpu.VMEM((n_blk, 8, rows), jnp.int32),
            pltpu.VMEM((8, tokens), f32),
            pltpu.VMEM((n_blk, rows, rows), f32),
            pltpu.VMEM((n_blk, 3, rows, LANES), bf16),
            pltpu.VMEM((3, tokens, LANES), bf16),
            pltpu.VMEM((n_blk, 2 * rows, 1), f32),
            pltpu.VMEM((n_blk, 2 * rows, 1), f32),
            pltpu.VMEM((n_blk, 2 * rows, LANES), f32),
            pltpu.VMEM((n_blk, rows, LANES), bf16),
            pltpu.VMEM((n_blk, rows, LANES), bf16),
            pltpu.VMEM((rows, width // 2), bf16),
            pltpu.VMEM((rows, model), f32),
            pltpu.VMEM((n_out, rows, OUT_CHUNK), bf16),
            pltpu.VMEM((n_out, rows // 2, OUT_CHUNK), bf16),
            dma((2,)),
            dma((3 * n_blk // 2,)),
            dma,
            dma((2,)),
            dma((n_blk,)),
            dma((n_blk,)),
            dma((2 * n_blk,)),
            dma((2 * n_blk,)),
            dma((3 * n_blk,)),
            dma((3 * n_blk,)),
            dma((n_blk,)),
            dma((n_blk,)),
            dma((n_out,)),
            dma((n_out,)),
        ],
        compiler_params=pltpu.CompilerParams(
            collective_id=0, has_side_effects=True, vmem_limit_bytes=56 * 1024 * 1024
        ),
    )(
        hidden_in,
        norm_gain[None, :],
        jnp.transpose(w_qkv, (1, 0, 2)),
        w_out,
        prefix_kv,
        segment,
        inverse,
    )
    return deliver(attended, stacked)


def deliver_kernel(attended_ref, stacked_ref, out_ref, kv_ref, sem):
    copies = []
    for n, (source, target) in enumerate(((stacked_ref, kv_ref), (attended_ref, out_ref))):
        share = source.shape[0] // DELIVER
        for i in range(DELIVER):
            part = pl.ds(i * share, share)
            copy = pltpu.make_async_copy(source.at[part], target.at[part], sem.at[n, i])
            copy.start()
            copies.append(copy)
    for copy in copies:
        copy.wait()


def deliver(attended, stacked):
    anywhere = pl.BlockSpec(memory_space=pl.ANY)
    inside = pl.BlockSpec(memory_space=pltpu.VMEM)
    return pl.pallas_call(
        deliver_kernel,
        name="deliver",
        out_shape=(
            jax.ShapeDtypeStruct(attended.shape, attended.dtype),
            jax.ShapeDtypeStruct(stacked.shape, stacked.dtype),
        ),
        in_specs=[inside, inside],
        out_specs=(anywhere, anywhere),
        scratch_shapes=[pltpu.SemaphoreType.DMA((2, DELIVER))],
    )(
        pltpu.with_memory_space_constraint(attended, pltpu.VMEM),
        pltpu.with_memory_space_constraint(stacked, pltpu.VMEM),
    )


def by_heads(hidden_in, norm_gain, w_qkv, w_out, prefix_kv, segment):
    rows, half = hidden_in.shape
    n_blk = lax.axis_size("blk")
    fits = (
        lax.axis_size("grp") == 2
        and lax.axis_size("tp") == 2
        and n_blk == 8
        and w_qkv.shape[2] == n_blk * LANES
        and rows == LANES
        and half % OUT_CHUNK == 0
        and prefix_kv.shape[0] % 16 == 0
    )
    form = on_device_heads if fits else on_device
    return form(hidden_in, norm_gain, w_qkv, w_out, prefix_kv, segment)


def solution(mesh):
    placed = (
        P(("grp", "blk"), "tp"),
        P(),
        P(None, None, "tp"),
        P("tp", None),
        P(("grp", "blk"), None, "tp"),
        P("grp", "blk"),
    )
    return jax.shard_map(
        by_heads,
        mesh=mesh,
        in_specs=placed,
        out_specs=(P(("grp", "blk", "tp"), None), P(("grp", "blk"), None, "tp")),
        check_vma=False,
    )
```

```python
import math

import jax
import jax.numpy as jnp
import numpy as np
from jax import lax
from jax.experimental import pallas as pl
from jax.experimental.pallas import tpu as pltpu
from jax.sharding import PartitionSpec as P

HD = 64
REQS = 8


def layer_norm(matrix_rows, norm_gain):
    values_f = matrix_rows.astype(jnp.float32)
    row_mean = jnp.mean(values_f, axis=-1, keepdims=True)
    centered = values_f - row_mean
    variance = jnp.mean(centered * centered, axis=-1, keepdims=True)
    return (centered * lax.rsqrt(variance + 1e-05) * norm_gain).astype(jnp.bfloat16)


def rotary(heads_f, positions):
    head_size = heads_f.shape[-1]
    rotated = head_size // 4
    half_rot = rotated // 2
    inverse = 10000.0 ** (-(jnp.arange(half_rot, dtype=jnp.float32) * 2.0) / rotated)
    angles = positions[:, None] * inverse[None, :]
    cos_table = jnp.cos(angles)[:, None, :]
    sine_table = jnp.sin(angles)[:, None, :]
    first_half = heads_f[..., :half_rot]
    second_half = heads_f[..., half_rot:rotated]
    return jnp.concatenate(
        [
            first_half * cos_table - second_half * sine_table,
            second_half * cos_table + first_half * sine_table,
            heads_f[..., rotated:],
        ],
        axis=-1,
    )


def attend_block(carried, queries, block_kv, visible, score_scale):
    maxima, totals, accumulated = carried
    key_count = block_kv.shape[0]
    head_count = queries.shape[1]
    block_keys = block_kv[:, 0].reshape(key_count, head_count, HD)
    block_values = block_kv[:, 1].reshape(key_count, head_count, HD)
    scores = (
        jnp.einsum("qhd,khd->qhk", queries, block_keys, preferred_element_type=jnp.float32)
        * score_scale
    )
    if visible is not None:
        scores = jnp.where(visible[:, None, :], scores, jnp.float32(-1e30))
    newest = jnp.maximum(maxima, jnp.max(scores, axis=-1))
    weights = jnp.exp(scores - newest[..., None])
    if visible is not None:
        weights = jnp.where(visible[:, None, :], weights, jnp.float32(0.0))
    factor = jnp.exp(maxima - newest)
    totals = totals * factor + jnp.sum(weights, axis=-1)
    accumulated = accumulated * factor[..., None] + jnp.einsum(
        "qhk,khd->qhd",
        weights.astype(jnp.bfloat16),
        block_values,
        preferred_element_type=jnp.float32,
    )
    return (newest, totals, accumulated)


def on_device(hidden_in, norm_gain, w_qkv, w_out, prefix_kv, segment):
    row_count = hidden_in.shape[0]
    local_width = w_qkv.shape[2]
    head_count = local_width // HD
    gathered = lax.all_gather(hidden_in, "tp", axis=1, tiled=True)
    normed = layer_norm(gathered, norm_gain)
    projected = jnp.einsum("td,dce->tce", normed, w_qkv, preferred_element_type=jnp.float32)
    seg_row = segment[0]
    labels = jnp.arange(REQS, dtype=jnp.int32)
    onehot = (seg_row[:, None] == labels[None, :]).astype(jnp.int32)
    counts = jnp.sum(onehot, axis=0)
    all_counts = lax.all_gather(counts[None, :], "blk", axis=0, tiled=True)
    request_sizes = jnp.sum(all_counts, axis=0)
    request_ends = jnp.sum(
        jnp.where(labels[None, :] <= labels[:, None], request_sizes[None, :], 0), axis=1
    )
    request_starts = request_ends - request_sizes
    cycle_size = lax.axis_size("blk")
    cycle_place = lax.axis_index("blk")
    row_index = jnp.arange(row_count, dtype=jnp.int32)
    query_index = cycle_place * row_count + row_index
    within = query_index - jnp.sum(onehot * request_starts[None, :], axis=1)
    prefix_len = prefix_kv.shape[0] * lax.axis_size("grp") * cycle_size
    positions = within.astype(jnp.float32) + float(prefix_len)
    queries = rotary(projected[:, 0].reshape(row_count, head_count, HD), positions).astype(
        jnp.bfloat16
    )
    key_heads = rotary(projected[:, 1].reshape(row_count, head_count, HD), positions).astype(
        jnp.bfloat16
    )
    values = projected[:, 2].astype(jnp.bfloat16)
    keys_values = jnp.stack([key_heads.reshape(row_count, local_width), values], axis=1)
    score_scale = 1.0 / math.sqrt(HD)
    running = (
        jnp.full((row_count, head_count), -1e30, jnp.float32),
        jnp.zeros((row_count, head_count), jnp.float32),
        jnp.zeros((row_count, head_count, HD), jnp.float32),
    )
    running = attend_block(
        running,
        queries,
        lax.all_gather(prefix_kv, ("grp", "blk"), axis=0, tiled=True),
        None,
        score_scale,
    )
    block_kv = lax.all_gather(keys_values, "blk", axis=0, tiled=True)
    key_index = jnp.arange(block_kv.shape[0], dtype=jnp.int32)
    key_segment = jnp.sum((key_index[:, None] >= request_ends[None, :]).astype(jnp.int32), axis=1)
    visible = (
        (key_segment[None, :] == seg_row[:, None])
        & (key_index[None, :] <= query_index[:, None])
        & True
    )

    def take_block(kept):
        return attend_block(kept, queries, block_kv, visible, score_scale)

    def skip_block(kept):
        return kept

    running = lax.cond(jnp.any(visible), take_block, skip_block, running)
    maxima, totals, accumulated = running
    attention = (
        (accumulated / totals[..., None]).astype(jnp.bfloat16).reshape(row_count, local_width)
    )
    attended = lax.psum_scatter(
        jnp.dot(attention, w_out, preferred_element_type=jnp.float32).astype(jnp.bfloat16),
        "tp",
        scatter_dimension=0,
        tiled=True,
    )
    return (attended, keys_values)


LANES = 128
OUT_CHUNK = 512
DELIVER = 2
MESH = pl.DeviceIdType.MESH


def head_pairs(block):
    wide = block.astype(jnp.float32)
    lane = lax.broadcasted_iota(jnp.int32, wide.shape, 1)
    first = jnp.where(lane < HD, wide, 0.0)
    second = jnp.where(lane < HD, 0.0, wide)
    return jnp.concatenate([first, second], axis=0).astype(jnp.bfloat16)


def attend_step(stacked, keys, values, mask, state):
    factor = math.log2(math.e) / math.sqrt(HD)
    scores = lax.dot_general(
        stacked, keys, (((1,), (1,)), ((), ())), preferred_element_type=jnp.float32
    )
    if mask is not None:
        rows = mask.shape[0]
        scores = jnp.concatenate(
            [
                jnp.where(mask, scores[:rows], jnp.float32(-1e30)),
                jnp.where(mask, scores[rows:], jnp.float32(-1e30)),
            ],
            axis=0,
        )
    top = jnp.max(scores, axis=1, keepdims=True)
    if state is not None:
        top = jnp.maximum(top, state[0])
    weights = jnp.exp2((scores - top) * factor)
    total = jnp.sum(weights, axis=1, keepdims=True)
    summed = jnp.dot(weights.astype(jnp.bfloat16), values, preferred_element_type=jnp.float32)
    if state is not None:
        shrink = jnp.exp2((state[0] - top) * factor)
        total = total + state[1] * shrink
        summed = summed + state[2] * shrink
    return top, total, summed


def block_kernel(
    n_blk,
    hid_ref,
    gain_ref,
    w_ref,
    wo_ref,
    pre_ref,
    seg_ref,
    inv_ref,
    out_ref,
    kv_ref,
    wbuf,
    wobuf,
    hid_mine,
    hid_other,
    pre_mine,
    normed,
    pre_out,
    pre_all,
    seg_out,
    seg_all,
    seg_flat,
    seg_col,
    send_buf,
    qkv,
    top_s,
    total_s,
    sum_s,
    obuf,
    attn_in,
    attn,
    low,
    part,
    part_other,
    in_sem,
    w_sem,
    wo_sem,
    hid_sem,
    seg_send,
    seg_recv,
    pre_send,
    pre_recv,
    qkv_send,
    qkv_recv,
    o_send,
    o_recv,
    part_send,
    part_recv,
):
    g, b, t = lax.axis_index("grp"), lax.axis_index("blk"), lax.axis_index("tp")
    rows, half = hid_mine.shape
    model = 2 * half
    pre_rows = pre_mine.shape[0]
    n_z = n_blk // 2
    near = n_blk // 2
    z, x = b // 2, b % 2
    side = z // 2
    near_base, far_base = side * near, (1 - side) * near
    partner = (g, b, 1 - t)
    across = (1 - g, b, t)

    def dest_z(i):
        if i < 2:
            return (1 - side) * (n_z - 1 - i) + side * i
        return side * 2 + (z % 2 + n_z - 1 - i) % 2

    def dest(n):
        return dest_z(n // 2) * 2 + (x + 1 + n) % 2

    def lanes(block):
        return pl.ds(pl.multiple_of(block * LANES, LANES), LANES)

    def token_rows(block):
        return pl.ds(pl.multiple_of(block * rows, rows), rows)

    barrier = pltpu.get_barrier_semaphore()
    pl.semaphore_signal(barrier, inc=1, device_id=partner, device_id_type=MESH)
    pl.semaphore_signal(barrier, inc=1, device_id=across, device_id_type=MESH)
    for n in range(n_blk - 1):
        pl.semaphore_signal(barrier, inc=1, device_id=(g, dest(n), t), device_id_type=MESH)

    pre_load = pltpu.make_async_copy(pre_ref, pre_mine, in_sem.at[0])
    pre_load.start()
    hid_load = pltpu.make_async_copy(hid_ref, hid_mine, in_sem.at[1])
    hid_load.start()
    pre_load.wait()
    hid_load.wait()

    def w_cols(i):
        return pl.ds(pl.multiple_of(dest_z(i) * 2 * LANES, 2 * LANES), 2 * LANES)

    def w_load(c, i):
        return pltpu.make_async_copy(
            w_ref.at[c, :, w_cols(i)], wbuf.at[i, c], w_sem.at[c * n_z + i]
        )

    for c in (2, 0, 1):
        for i in range(n_z):
            w_load(c, i).start()
    wo_copy = pltpu.make_async_copy(wo_ref, wobuf, wo_sem)
    wo_copy.start()

    seg_out[...] = jnp.broadcast_to(seg_ref[...], seg_out.shape)
    for d in range(n_blk):
        for c in range(2):
            pre_out[d, c] = pre_mine[:, c, d * LANES : (d + 1) * LANES]
    pl.semaphore_wait(barrier, n_blk + 1)

    hid_copy = pltpu.make_async_remote_copy(
        hid_mine, hid_other, hid_sem.at[0], hid_sem.at[1], device_id=partner, device_id_type=MESH
    )
    hid_copy.start()

    def seg_copy(n, slot):
        return pltpu.make_async_remote_copy(
            seg_out,
            seg_all.at[slot],
            seg_send.at[n],
            seg_recv.at[slot],
            device_id=(g, dest(n), t),
            device_id_type=MESH,
        )

    for n in range(n_blk - 1):
        seg_copy(n, b).start()

    def pre_slot(slot):
        return pre_all.at[:, pl.ds(pl.multiple_of(slot * pre_rows, pre_rows), pre_rows), :]

    def pre_copy(n, slot):
        return pltpu.make_async_remote_copy(
            pre_out.at[dest(n)],
            pre_slot(slot),
            pre_send.at[n],
            pre_recv.at[slot],
            device_id=(g, dest(n), t),
            device_id_type=MESH,
        )

    def forward_copy(n, slot):
        return pltpu.make_async_remote_copy(
            pre_slot(slot),
            pre_slot(slot),
            pre_send.at[n_blk + n],
            pre_recv.at[slot],
            device_id=across,
            device_id_type=MESH,
        )

    my_slot = g * n_blk + b
    for n in range(n_blk - 1):
        pre_copy(n, my_slot).start()
    pre_all[:, pl.ds(pl.multiple_of(my_slot * pre_rows, pre_rows), pre_rows), :] = pre_out[b]
    forward_copy(n_blk - 1, my_slot).start()
    seg_all[b] = seg_out[...]

    def pass_on(numbers):
        for n in numbers:
            slot = g * n_blk + dest(n)
            pre_copy(n, slot).wait_recv()
            forward_copy(n, slot).start()

    mine = hid_mine[...].astype(jnp.float32)
    mine_sum = jnp.sum(mine, axis=1, keepdims=True)
    hid_copy.wait()
    other = hid_other[...].astype(jnp.float32)
    mean = (mine_sum + jnp.sum(other, axis=1, keepdims=True)) * (1.0 / model)
    mine = mine - mean
    other = other - mean
    variance = (
        jnp.sum(mine * mine, axis=1, keepdims=True)
        + jnp.sum(other * other, axis=1, keepdims=True)
    ) * (1.0 / model)
    scale = lax.rsqrt(variance + 1e-05)
    mine_cols = pl.ds(pl.multiple_of(t * half, half), half)
    other_cols = pl.ds(pl.multiple_of((1 - t) * half, half), half)
    normed[:, mine_cols] = (mine * scale * gain_ref[:, mine_cols]).astype(jnp.bfloat16)
    normed[:, other_cols] = (other * scale * gain_ref[:, other_cols]).astype(jnp.bfloat16)

    def qkv_copy(c, n, slot):
        return pltpu.make_async_remote_copy(
            send_buf.at[n, c],
            qkv.at[c, token_rows(slot), :],
            qkv_send.at[c * n_blk + n],
            qkv_recv.at[c * n_blk + slot],
            device_id=(g, dest(n), t),
            device_id_type=MESH,
        )

    def start_others(c, i):
        for n in (2 * i, 2 * i + 1):
            if n < n_blk - 1:
                qkv_copy(c, n, b).start()

    for i in range(n_z):
        w_load(2, i).wait()
        product = jnp.dot(normed[...], wbuf[i, 2], preferred_element_type=jnp.float32)
        for h in range(2):
            tile = product[:, h * LANES : (h + 1) * LANES].astype(jnp.bfloat16)
            send_buf[2 * i + (x + 1 + h) % 2, 2] = tile
            kv_ref[:, 1, lanes(dest_z(i) * 2 + h)] = tile
        start_others(2, i)

    for n in range(n_blk - 1):
        seg_copy(n, dest(n)).wait_recv()
    for c in range(n_blk):
        row = seg_all[c].astype(jnp.float32)
        seg_flat[:, c * rows : (c + 1) * rows] = row
        seg_col[c] = jnp.broadcast_to(row[:1], (rows, rows)).T
    own_seg = seg_col[b][:, :1]
    before = jnp.where(seg_flat[:1] < own_seg, 1.0, 0.0)
    start = jnp.sum(before, axis=1, keepdims=True)
    row_iota = lax.broadcasted_iota(jnp.int32, (rows, LANES), 0)
    prefix_len = float(2 * n_blk * pre_rows)
    position = (b * rows + row_iota).astype(jnp.float32) - start + prefix_len
    angles = position * inv_ref[:1]
    in_head = lax.broadcasted_iota(jnp.int32, (rows, LANES), 1) % HD
    rotated = HD // 4
    sine = jnp.sin(angles)
    cos_t = jnp.where(in_head < rotated, jnp.cos(angles), 1.0)
    low_t = jnp.where(in_head < rotated // 2, -sine, 0.0)
    high_t = jnp.where((in_head >= rotated // 2) & (in_head < rotated), sine, 0.0)


    for m in range(2 * n_z):
        c, i = m // n_z, m % n_z
        w_load(c, i).wait()
        product = jnp.dot(normed[...], wbuf[i, c], preferred_element_type=jnp.float32)
        for h in range(2):
            tile = product[:, h * LANES : (h + 1) * LANES]
            tile = (
                tile * cos_t
                + pltpu.roll(tile, LANES - rotated // 2, 1) * low_t
                + pltpu.roll(tile, rotated // 2, 1) * high_t
            ).astype(jnp.bfloat16)
            send_buf[2 * i + (x + 1 + h) % 2, c] = tile
            if c == 1:
                kv_ref[:, 0, lanes(dest_z(i) * 2 + h)] = tile
        if c == 0 or i != 1:
            start_others(c, i)

    qkv[:, token_rows(b), :] = send_buf[n_blk - 1]
    pass_on((6, 5, 4, 3, 2, 1, 0))

    for c in range(n_blk):
        forward_copy(c, (1 - g) * n_blk + c).wait_recv()

    split = near * rows

    def o_copy(block, slot):
        return pltpu.make_async_remote_copy(
            obuf.at[block],
            attn_in.at[slot],
            o_send.at[block],
            o_recv.at[slot],
            device_id=(g, block, t),
            device_id_type=MESH,
        )

    def arrive(c, block):
        qkv_copy(c, 0, block).wait_recv()

    def queries(block):
        return head_pairs(qkv[0, token_rows(block), :])

    def prefix_step(block):
        return attend_step(queries(block), pre_all[0], pre_all[1], None, None)

    def half_step(block, c, state):
        q_seg = seg_col[block][:, :1]
        q_index = block * rows + lax.broadcasted_iota(jnp.int32, (rows, split), 0)
        k_index = c * split + lax.broadcasted_iota(jnp.int32, (rows, split), 1)
        keys = pl.ds(pl.multiple_of(c * split, split), split)
        mask = (seg_flat[pl.ds(0, 1), keys] == q_seg) & (k_index <= q_index)
        return attend_step(queries(block), qkv[1, keys, :], qkv[2, keys, :], mask, state)

    def keep(block, state):
        top_s[block], total_s[block], sum_s[block] = state

    def kept(block):
        return top_s[block], total_s[block], sum_s[block]

    def finish(blocks, states):
        lane = lax.broadcasted_iota(jnp.int32, (rows, LANES), 1)
        for block, (_, total, summed) in zip(blocks, states):
            result = summed / total
            obuf[block] = jnp.where(lane < HD, result[:rows], result[rows:]).astype(jnp.bfloat16)
        for block in blocks:

            @pl.when(block != b)
            def _():
                o_copy(block, b).start()

    for n in range(near, n_blk - 1):
        for c in range(3):
            arrive(c, dest(n))

    @pl.loop(0, near // 2)
    def _(m):
        @pl.when(m == 1)
        def _():
            start_others(1, 1)

        blocks = (near_base + 2 * m, near_base + 2 * m + 1)
        states = [half_step(c, side, prefix_step(c)) for c in blocks]

        @pl.when(side == 0)
        def _():
            finish(blocks, states)

        @pl.when(side == 1)
        def _():
            for c, state in zip(blocks, states):
                keep(c, state)

    @pl.loop(0, near // 2)
    def _(m):
        blocks = (far_base + 2 * m, far_base + 2 * m + 1)
        for c in blocks:
            arrive(0, c)
        for c, state in zip(blocks, [prefix_step(c) for c in blocks]):
            keep(c, state)

        @pl.when(side == 0)
        def _():
            for c, state in zip(blocks, [half_step(c, 0, kept(c)) for c in blocks]):
                keep(c, state)

    for m in range(near):
        arrive(2, far_base + m)
        arrive(1, far_base + m)

    @pl.loop(0, (1 + side) * (near // 2))
    def _(m):
        first = (far_base + 2 * m) % n_blk
        blocks = (first, first + 1)
        finish(blocks, [half_step(c, 1 - side, kept(c)) for c in blocks])

    attn_in[b] = obuf[b]
    wo_copy.wait()

    def arrived(first, count):
        for m in range(count):

            @pl.when(first + m != b)
            def _():
                o_copy(0, first + m).wait_recv()

        return jnp.concatenate([attn_in[first + m] for m in range(count)], axis=1)

    def wo_rows(first, count):
        return pl.ds(pl.multiple_of(first * LANES, count * LANES), count * LANES)

    n_out = model // OUT_CHUNK

    def columns(j):
        return pl.ds(pl.multiple_of(j * OUT_CHUNK, OUT_CHUNK), OUT_CHUNK)

    near_rows, far_rows = wo_rows(near_base, near), wo_rows(far_base, near)
    attn[...] = arrived(near_base, near)

    @pl.loop(0, n_out)
    def _(j):
        low[:, columns(j)] = jnp.dot(
            attn[...], wobuf[near_rows, columns(j)], preferred_element_type=jnp.float32
        )

    attn[...] = arrived(far_base, near)

    share = rows // 2
    mine_rows = pl.ds(pl.multiple_of(t * share, share), share)
    other_rows = pl.ds(pl.multiple_of((1 - t) * share, share), share)

    def part_copy(j):
        return pltpu.make_async_remote_copy(
            part.at[j, other_rows, :],
            part_other.at[j],
            part_send.at[j],
            part_recv.at[j],
            device_id=partner,
            device_id_type=MESH,
        )

    @pl.loop(0, n_out)
    def _(j):
        product = low[:, columns(j)] + jnp.dot(
            attn[...], wobuf[far_rows, columns(j)], preferred_element_type=jnp.float32
        )
        part[j] = product.astype(jnp.bfloat16)
        part_copy(j).start()

    for j in range(n_out):
        part_copy(j).wait_recv()
        out_ref[:, j * OUT_CHUNK : (j + 1) * OUT_CHUNK] = (
            part[j, mine_rows, :].astype(jnp.float32) + part_other[j].astype(jnp.float32)
        ).astype(jnp.bfloat16)

    for j in range(n_out):
        part_copy(j).wait_send()
    for n in range(n_blk):

        if n < n_blk - 1:
            for c in range(3):
                qkv_copy(c, n, b).wait_send()
            o_copy(dest(n), b).wait_send()
        forward_copy(n, my_slot).wait_send()
    for n in range(n_blk - 1):
        seg_copy(n, b).wait_send()
        pre_copy(n, my_slot).wait_send()


def on_device_heads(hidden_in, norm_gain, w_qkv, w_out, prefix_kv, segment):
    rows, half = hidden_in.shape
    model = 2 * half
    width = w_qkv.shape[2]
    n_blk = width // LANES
    tokens = n_blk * rows
    pre_rows = prefix_kv.shape[0]
    rotated = HD // 4
    inverse = 10000.0 ** (-(np.arange(rotated // 2) * 2.0) / rotated)
    inverse = jnp.asarray(np.tile(inverse, (8, LANES // (rotated // 2))), jnp.float32)
    vmem = pl.BlockSpec(memory_space=pltpu.VMEM)
    hbm = pl.BlockSpec(memory_space=pl.ANY)
    bf16, f32 = jnp.bfloat16, jnp.float32
    dma = pltpu.SemaphoreType.DMA
    n_out = model // OUT_CHUNK

    def kernel(*refs):
        block_kernel(n_blk, *refs)

    attended, stacked = pl.pallas_call(
        kernel,
        name="attention_block",
        out_shape=(
            pltpu.VMEM((rows // 2, model), bf16),
            pltpu.VMEM((rows, 2, width), bf16),
        ),
        in_specs=[hbm, vmem, hbm, hbm, hbm, vmem, vmem],
        out_specs=(vmem, vmem),
        scratch_shapes=[
            pltpu.VMEM((n_blk // 2, 3, model, 2 * LANES), bf16),
            pltpu.VMEM((width, model), bf16),
            pltpu.VMEM((rows, half), bf16),
            pltpu.VMEM((rows, half), bf16),
            pltpu.VMEM((pre_rows, 2, width), bf16),
            pltpu.VMEM((rows, model), bf16),
            pltpu.VMEM((n_blk, 2, pre_rows, LANES), bf16),
            pltpu.VMEM((2, 2 * n_blk * pre_rows, LANES), bf16),
            pltpu.VMEM((8, rows), jnp.int32),
            pltpu.VMEM((n_blk, 8, rows), jnp.int32),
            pltpu.VMEM((8, tokens), f32),
            pltpu.VMEM((n_blk, rows, rows), f32),
            pltpu.VMEM((n_blk, 3, rows, LANES), bf16),
            pltpu.VMEM((3, tokens, LANES), bf16),
            pltpu.VMEM((n_blk, 2 * rows, 1), f32),
            pltpu.VMEM((n_blk, 2 * rows, 1), f32),
            pltpu.VMEM((n_blk, 2 * rows, LANES), f32),
            pltpu.VMEM((n_blk, rows, LANES), bf16),
            pltpu.VMEM((n_blk, rows, LANES), bf16),
            pltpu.VMEM((rows, width // 2), bf16),
            pltpu.VMEM((rows, model), f32),
            pltpu.VMEM((n_out, rows, OUT_CHUNK), bf16),
            pltpu.VMEM((n_out, rows // 2, OUT_CHUNK), bf16),
            dma((2,)),
            dma((3 * n_blk // 2,)),
            dma,
            dma((2,)),
            dma((n_blk,)),
            dma((n_blk,)),
            dma((2 * n_blk,)),
            dma((2 * n_blk,)),
            dma((3 * n_blk,)),
            dma((3 * n_blk,)),
            dma((n_blk,)),
            dma((n_blk,)),
            dma((n_out,)),
            dma((n_out,)),
        ],
        compiler_params=pltpu.CompilerParams(
            collective_id=0, has_side_effects=True, vmem_limit_bytes=56 * 1024 * 1024
        ),
    )(
        hidden_in,
        norm_gain[None, :],
        jnp.transpose(w_qkv, (1, 0, 2)),
        w_out,
        prefix_kv,
        segment,
        inverse,
    )
    return deliver(attended, stacked)


def deliver_kernel(attended_ref, stacked_ref, out_ref, kv_ref, sem):
    copies = []
    for n, (source, target) in enumerate(((stacked_ref, kv_ref), (attended_ref, out_ref))):
        share = source.shape[0] // DELIVER
        for i in range(DELIVER):
            part = pl.ds(i * share, share)
            copy = pltpu.make_async_copy(source.at[part], target.at[part], sem.at[n, i])
            copy.start()
            copies.append(copy)
    for copy in copies:
        copy.wait()


def deliver(attended, stacked):
    anywhere = pl.BlockSpec(memory_space=pl.ANY)
    inside = pl.BlockSpec(memory_space=pltpu.VMEM)
    return pl.pallas_call(
        deliver_kernel,
        name="deliver",
        out_shape=(
            jax.ShapeDtypeStruct(attended.shape, attended.dtype),
            jax.ShapeDtypeStruct(stacked.shape, stacked.dtype),
        ),
        in_specs=[inside, inside],
        out_specs=(anywhere, anywhere),
        scratch_shapes=[pltpu.SemaphoreType.DMA((2, DELIVER))],
    )(
        pltpu.with_memory_space_constraint(attended, pltpu.VMEM),
        pltpu.with_memory_space_constraint(stacked, pltpu.VMEM),
    )


def by_heads(hidden_in, norm_gain, w_qkv, w_out, prefix_kv, segment):
    rows, half = hidden_in.shape
    n_blk = lax.axis_size("blk")
    fits = (
        lax.axis_size("grp") == 2
        and lax.axis_size("tp") == 2
        and n_blk == 8
        and w_qkv.shape[2] == n_blk * LANES
        and rows == LANES
        and half % OUT_CHUNK == 0
        and prefix_kv.shape[0] % 16 == 0
    )
    form = on_device_heads if fits else on_device
    return form(hidden_in, norm_gain, w_qkv, w_out, prefix_kv, segment)


def solution(mesh):
    placed = (
        P(("grp", "blk"), "tp"),
        P(),
        P(None, None, "tp"),
        P("tp", None),
        P(("grp", "blk"), None, "tp"),
        P("grp", "blk"),
    )
    return jax.shard_map(
        by_heads,
        mesh=mesh,
        in_specs=placed,
        out_specs=(P(("grp", "blk", "tp"), None), P(("grp", "blk"), None, "tp")),
        check_vma=False,
    )
```

```python
import math

import jax
import jax.numpy as jnp
import numpy as np
from jax import lax
from jax.experimental import pallas as pl
from jax.experimental.pallas import tpu as pltpu
from jax.sharding import PartitionSpec as P

HD = 64
REQS = 8


def layer_norm(matrix_rows, norm_gain):
    values_f = matrix_rows.astype(jnp.float32)
    row_mean = jnp.mean(values_f, axis=-1, keepdims=True)
    centered = values_f - row_mean
    variance = jnp.mean(centered * centered, axis=-1, keepdims=True)
    return (centered * lax.rsqrt(variance + 1e-05) * norm_gain).astype(jnp.bfloat16)


def rotary(heads_f, positions):
    head_size = heads_f.shape[-1]
    rotated = head_size // 4
    half_rot = rotated // 2
    inverse = 10000.0 ** (-(jnp.arange(half_rot, dtype=jnp.float32) * 2.0) / rotated)
    angles = positions[:, None] * inverse[None, :]
    cos_table = jnp.cos(angles)[:, None, :]
    sine_table = jnp.sin(angles)[:, None, :]
    first_half = heads_f[..., :half_rot]
    second_half = heads_f[..., half_rot:rotated]
    return jnp.concatenate(
        [
            first_half * cos_table - second_half * sine_table,
            second_half * cos_table + first_half * sine_table,
            heads_f[..., rotated:],
        ],
        axis=-1,
    )


def attend_block(carried, queries, block_kv, visible, score_scale):
    maxima, totals, accumulated = carried
    key_count = block_kv.shape[0]
    head_count = queries.shape[1]
    block_keys = block_kv[:, 0].reshape(key_count, head_count, HD)
    block_values = block_kv[:, 1].reshape(key_count, head_count, HD)
    scores = (
        jnp.einsum("qhd,khd->qhk", queries, block_keys, preferred_element_type=jnp.float32)
        * score_scale
    )
    if visible is not None:
        scores = jnp.where(visible[:, None, :], scores, jnp.float32(-1e30))
    newest = jnp.maximum(maxima, jnp.max(scores, axis=-1))
    weights = jnp.exp(scores - newest[..., None])
    if visible is not None:
        weights = jnp.where(visible[:, None, :], weights, jnp.float32(0.0))
    factor = jnp.exp(maxima - newest)
    totals = totals * factor + jnp.sum(weights, axis=-1)
    accumulated = accumulated * factor[..., None] + jnp.einsum(
        "qhk,khd->qhd",
        weights.astype(jnp.bfloat16),
        block_values,
        preferred_element_type=jnp.float32,
    )
    return (newest, totals, accumulated)


def on_device(hidden_in, norm_gain, w_qkv, w_out, prefix_kv, segment):
    row_count = hidden_in.shape[0]
    local_width = w_qkv.shape[2]
    head_count = local_width // HD
    gathered = lax.all_gather(hidden_in, "tp", axis=1, tiled=True)
    normed = layer_norm(gathered, norm_gain)
    projected = jnp.einsum("td,dce->tce", normed, w_qkv, preferred_element_type=jnp.float32)
    seg_row = segment[0]
    labels = jnp.arange(REQS, dtype=jnp.int32)
    onehot = (seg_row[:, None] == labels[None, :]).astype(jnp.int32)
    counts = jnp.sum(onehot, axis=0)
    all_counts = lax.all_gather(counts[None, :], "blk", axis=0, tiled=True)
    request_sizes = jnp.sum(all_counts, axis=0)
    request_ends = jnp.sum(
        jnp.where(labels[None, :] <= labels[:, None], request_sizes[None, :], 0), axis=1
    )
    request_starts = request_ends - request_sizes
    cycle_size = lax.axis_size("blk")
    cycle_place = lax.axis_index("blk")
    row_index = jnp.arange(row_count, dtype=jnp.int32)
    query_index = cycle_place * row_count + row_index
    within = query_index - jnp.sum(onehot * request_starts[None, :], axis=1)
    prefix_len = prefix_kv.shape[0] * lax.axis_size("grp") * cycle_size
    positions = within.astype(jnp.float32) + float(prefix_len)
    queries = rotary(projected[:, 0].reshape(row_count, head_count, HD), positions).astype(
        jnp.bfloat16
    )
    key_heads = rotary(projected[:, 1].reshape(row_count, head_count, HD), positions).astype(
        jnp.bfloat16
    )
    values = projected[:, 2].astype(jnp.bfloat16)
    keys_values = jnp.stack([key_heads.reshape(row_count, local_width), values], axis=1)
    score_scale = 1.0 / math.sqrt(HD)
    running = (
        jnp.full((row_count, head_count), -1e30, jnp.float32),
        jnp.zeros((row_count, head_count), jnp.float32),
        jnp.zeros((row_count, head_count, HD), jnp.float32),
    )
    running = attend_block(
        running,
        queries,
        lax.all_gather(prefix_kv, ("grp", "blk"), axis=0, tiled=True),
        None,
        score_scale,
    )
    block_kv = lax.all_gather(keys_values, "blk", axis=0, tiled=True)
    key_index = jnp.arange(block_kv.shape[0], dtype=jnp.int32)
    key_segment = jnp.sum((key_index[:, None] >= request_ends[None, :]).astype(jnp.int32), axis=1)
    visible = (
        (key_segment[None, :] == seg_row[:, None])
        & (key_index[None, :] <= query_index[:, None])
        & True
    )

    def take_block(kept):
        return attend_block(kept, queries, block_kv, visible, score_scale)

    def skip_block(kept):
        return kept

    running = lax.cond(jnp.any(visible), take_block, skip_block, running)
    maxima, totals, accumulated = running
    attention = (
        (accumulated / totals[..., None]).astype(jnp.bfloat16).reshape(row_count, local_width)
    )
    attended = lax.psum_scatter(
        jnp.dot(attention, w_out, preferred_element_type=jnp.float32).astype(jnp.bfloat16),
        "tp",
        scatter_dimension=0,
        tiled=True,
    )
    return (attended, keys_values)


LANES = 128
OUT_CHUNK = 512
DELIVER = 2
MESH = pl.DeviceIdType.MESH


def head_pairs(block):
    wide = block.astype(jnp.float32)
    lane = lax.broadcasted_iota(jnp.int32, wide.shape, 1)
    first = jnp.where(lane < HD, wide, 0.0)
    second = jnp.where(lane < HD, 0.0, wide)
    return jnp.concatenate([first, second], axis=0).astype(jnp.bfloat16)


def attend_step(stacked, keys, values, mask, state):
    factor = math.log2(math.e) / math.sqrt(HD)
    scores = lax.dot_general(
        stacked, keys, (((1,), (1,)), ((), ())), preferred_element_type=jnp.float32
    )
    if mask is not None:
        rows = mask.shape[0]
        scores = jnp.concatenate(
            [
                jnp.where(mask, scores[:rows], jnp.float32(-1e30)),
                jnp.where(mask, scores[rows:], jnp.float32(-1e30)),
            ],
            axis=0,
        )
    top = jnp.max(scores, axis=1, keepdims=True)
    if state is not None:
        top = jnp.maximum(top, state[0])
    weights = jnp.exp2((scores - top) * factor)
    total = jnp.sum(weights, axis=1, keepdims=True)
    summed = jnp.dot(weights.astype(jnp.bfloat16), values, preferred_element_type=jnp.float32)
    if state is not None:
        shrink = jnp.exp2((state[0] - top) * factor)
        total = total + state[1] * shrink
        summed = summed + state[2] * shrink
    return top, total, summed


def block_kernel(
    n_blk,
    hid_ref,
    gain_ref,
    w_ref,
    wo_ref,
    pre_ref,
    seg_ref,
    inv_ref,
    out_ref,
    kv_ref,
    wbuf,
    wobuf,
    hid_mine,
    hid_other,
    pre_mine,
    normed,
    pre_out,
    pre_all,
    seg_out,
    seg_all,
    seg_flat,
    seg_col,
    send_buf,
    qkv,
    top_s,
    total_s,
    sum_s,
    obuf,
    attn_in,
    attn,
    low,
    part,
    part_other,
    in_sem,
    w_sem,
    wo_sem,
    hid_sem,
    seg_send,
    seg_recv,
    pre_send,
    pre_recv,
    qkv_send,
    qkv_recv,
    o_send,
    o_recv,
    part_send,
    part_recv,
):
    g, b, t = lax.axis_index("grp"), lax.axis_index("blk"), lax.axis_index("tp")
    rows, half = hid_mine.shape
    model = 2 * half
    pre_rows = pre_mine.shape[0]
    n_z = n_blk // 2
    near = n_blk // 2
    z, x = b // 2, b % 2
    side = z // 2
    near_base, far_base = side * near, (1 - side) * near
    partner = (g, b, 1 - t)
    across = (1 - g, b, t)

    def dest_z(i):
        if i < 2:
            return (1 - side) * (n_z - 1 - i) + side * i
        return side * 2 + (z % 2 + n_z - 1 - i) % 2

    def dest(n):
        return dest_z(n // 2) * 2 + (x + 1 + n) % 2

    def lanes(block):
        return pl.ds(pl.multiple_of(block * LANES, LANES), LANES)

    def token_rows(block):
        return pl.ds(pl.multiple_of(block * rows, rows), rows)

    barrier = pltpu.get_barrier_semaphore()
    pl.semaphore_signal(barrier, inc=1, device_id=partner, device_id_type=MESH)
    pl.semaphore_signal(barrier, inc=1, device_id=across, device_id_type=MESH)
    for n in range(n_blk - 1):
        pl.semaphore_signal(barrier, inc=1, device_id=(g, dest(n), t), device_id_type=MESH)

    pre_load = pltpu.make_async_copy(pre_ref, pre_mine, in_sem.at[0])
    pre_load.start()
    hid_load = pltpu.make_async_copy(hid_ref, hid_mine, in_sem.at[1])
    hid_load.start()
    pre_load.wait()
    hid_load.wait()

    def w_cols(i):
        return pl.ds(pl.multiple_of(dest_z(i) * 2 * LANES, 2 * LANES), 2 * LANES)

    def w_load(c, i):
        return pltpu.make_async_copy(
            w_ref.at[c, :, w_cols(i)], wbuf.at[i, c], w_sem.at[c * n_z + i]
        )

    for c in (2, 0, 1):
        for i in range(n_z):
            w_load(c, (i + 2 * (c % 2)) % n_z).start()
    wo_copy = pltpu.make_async_copy(wo_ref, wobuf, wo_sem)
    wo_copy.start()

    seg_out[...] = jnp.broadcast_to(seg_ref[...], seg_out.shape)
    for d in range(n_blk):
        for c in range(2):
            pre_out[d, c] = pre_mine[:, c, d * LANES : (d + 1) * LANES]
    pl.semaphore_wait(barrier, n_blk + 1)

    hid_copy = pltpu.make_async_remote_copy(
        hid_mine, hid_other, hid_sem.at[0], hid_sem.at[1], device_id=partner, device_id_type=MESH
    )
    hid_copy.start()

    def seg_copy(n, slot):
        return pltpu.make_async_remote_copy(
            seg_out,
            seg_all.at[slot],
            seg_send.at[n],
            seg_recv.at[slot],
            device_id=(g, dest(n), t),
            device_id_type=MESH,
        )

    for n in range(n_blk - 1):
        seg_copy(n, b).start()

    def pre_slot(slot):
        return pre_all.at[:, pl.ds(pl.multiple_of(slot * pre_rows, pre_rows), pre_rows), :]

    def pre_copy(n, slot):
        return pltpu.make_async_remote_copy(
            pre_out.at[dest(n)],
            pre_slot(slot),
            pre_send.at[n],
            pre_recv.at[slot],
            device_id=(g, dest(n), t),
            device_id_type=MESH,
        )

    def forward_copy(n, slot):
        return pltpu.make_async_remote_copy(
            pre_slot(slot),
            pre_slot(slot),
            pre_send.at[n_blk + n],
            pre_recv.at[slot],
            device_id=across,
            device_id_type=MESH,
        )

    my_slot = g * n_blk + b
    for n in range(n_blk - 1):
        pre_copy(n, my_slot).start()
    pre_all[:, pl.ds(pl.multiple_of(my_slot * pre_rows, pre_rows), pre_rows), :] = pre_out[b]
    forward_copy(n_blk - 1, my_slot).start()
    seg_all[b] = seg_out[...]

    def pass_on(numbers):
        for n in numbers:
            slot = g * n_blk + dest(n)
            pre_copy(n, slot).wait_recv()
            forward_copy(n, slot).start()

    mine = hid_mine[...].astype(jnp.float32)
    mine_sum = jnp.sum(mine, axis=1, keepdims=True)
    hid_copy.wait()
    other = hid_other[...].astype(jnp.float32)
    mean = (mine_sum + jnp.sum(other, axis=1, keepdims=True)) * (1.0 / model)
    mine = mine - mean
    other = other - mean
    variance = (
        jnp.sum(mine * mine, axis=1, keepdims=True)
        + jnp.sum(other * other, axis=1, keepdims=True)
    ) * (1.0 / model)
    scale = lax.rsqrt(variance + 1e-05)
    mine_cols = pl.ds(pl.multiple_of(t * half, half), half)
    other_cols = pl.ds(pl.multiple_of((1 - t) * half, half), half)
    normed[:, mine_cols] = (mine * scale * gain_ref[:, mine_cols]).astype(jnp.bfloat16)
    normed[:, other_cols] = (other * scale * gain_ref[:, other_cols]).astype(jnp.bfloat16)

    def qkv_copy(c, n, slot):
        return pltpu.make_async_remote_copy(
            send_buf.at[n, c],
            qkv.at[c, token_rows(slot), :],
            qkv_send.at[c * n_blk + n],
            qkv_recv.at[c * n_blk + slot],
            device_id=(g, dest(n), t),
            device_id_type=MESH,
        )

    def start_others(c, i):
        for n in (2 * i, 2 * i + 1):
            if n < n_blk - 1:
                qkv_copy(c, n, b).start()

    for i in range(n_z):
        w_load(2, i).wait()
        product = jnp.dot(normed[...], wbuf[i, 2], preferred_element_type=jnp.float32)
        for h in range(2):
            tile = product[:, h * LANES : (h + 1) * LANES].astype(jnp.bfloat16)
            send_buf[2 * i + (x + 1 + h) % 2, 2] = tile
            kv_ref[:, 1, lanes(dest_z(i) * 2 + h)] = tile
        start_others(2, i)

    for n in range(n_blk - 1):
        seg_copy(n, dest(n)).wait_recv()
    for c in range(n_blk):
        row = seg_all[c].astype(jnp.float32)
        seg_flat[:, c * rows : (c + 1) * rows] = row
        seg_col[c] = jnp.broadcast_to(row[:1], (rows, rows)).T
    own_seg = seg_col[b][:, :1]
    before = jnp.where(seg_flat[:1] < own_seg, 1.0, 0.0)
    start = jnp.sum(before, axis=1, keepdims=True)
    row_iota = lax.broadcasted_iota(jnp.int32, (rows, LANES), 0)
    prefix_len = float(2 * n_blk * pre_rows)
    position = (b * rows + row_iota).astype(jnp.float32) - start + prefix_len
    angles = position * inv_ref[:1]
    in_head = lax.broadcasted_iota(jnp.int32, (rows, LANES), 1) % HD
    rotated = HD // 4
    sine = jnp.sin(angles)
    cos_t = jnp.where(in_head < rotated, jnp.cos(angles), 1.0)
    low_t = jnp.where(in_head < rotated // 2, -sine, 0.0)
    high_t = jnp.where((in_head >= rotated // 2) & (in_head < rotated), sine, 0.0)


    for m in range(2 * n_z):
        c = m // n_z
        i = m % n_z if c == 0 else (m + 2) % n_z
        w_load(c, i).wait()
        product = jnp.dot(normed[...], wbuf[i, c], preferred_element_type=jnp.float32)
        for h in range(2):
            tile = product[:, h * LANES : (h + 1) * LANES]
            tile = (
                tile * cos_t
                + pltpu.roll(tile, LANES - rotated // 2, 1) * low_t
                + pltpu.roll(tile, rotated // 2, 1) * high_t
            ).astype(jnp.bfloat16)
            send_buf[2 * i + (x + 1 + h) % 2, c] = tile
            if c == 1:
                kv_ref[:, 0, lanes(dest_z(i) * 2 + h)] = tile
        if c == 0 or i != 1:
            start_others(c, i)

    qkv[:, token_rows(b), :] = send_buf[n_blk - 1]
    pass_on((6, 5, 4, 3, 2, 1, 0))

    for c in range(n_blk):
        forward_copy(c, (1 - g) * n_blk + c).wait_recv()

    split = near * rows

    def o_copy(block, slot):
        return pltpu.make_async_remote_copy(
            obuf.at[block],
            attn_in.at[slot],
            o_send.at[block],
            o_recv.at[slot],
            device_id=(g, block, t),
            device_id_type=MESH,
        )

    def arrive(c, block):
        qkv_copy(c, 0, block).wait_recv()

    def queries(block):
        return head_pairs(qkv[0, token_rows(block), :])

    def prefix_step(block):
        return attend_step(queries(block), pre_all[0], pre_all[1], None, None)

    def half_step(block, c, state, count):
        q_seg = seg_col[block][:, :1]
        q_index = block * rows + lax.broadcasted_iota(jnp.int32, (rows, count), 0)
        k_index = c * split + lax.broadcasted_iota(jnp.int32, (rows, count), 1)
        keys = pl.ds(pl.multiple_of(c * split, split), count)
        mask = (seg_flat[pl.ds(0, 1), keys] == q_seg) & (k_index <= q_index)
        return attend_step(queries(block), qkv[1, keys, :], qkv[2, keys, :], mask, state)

    def keep(block, state):
        top_s[block], total_s[block], sum_s[block] = state

    def kept(block):
        return top_s[block], total_s[block], sum_s[block]

    def finish(blocks, states):
        lane = lax.broadcasted_iota(jnp.int32, (rows, LANES), 1)
        for block, (_, total, summed) in zip(blocks, states):
            result = summed / total
            obuf[block] = jnp.where(lane < HD, result[:rows], result[rows:]).astype(jnp.bfloat16)
        for block in blocks:

            @pl.when(block != b)
            def _():
                o_copy(block, b).start()

    for n in range(near, n_blk - 1):
        for c in range(3):
            arrive(c, dest(n))

    @pl.loop(0, near // 2)
    def _(m):
        @pl.when(m == 1)
        def _():
            start_others(1, 1)

        blocks = (near_base + 2 * m, near_base + 2 * m + 1)
        states = [half_step(c, side, prefix_step(c), split) for c in blocks]

        @pl.when(side == 0)
        def _():
            finish(blocks, states)

        @pl.when(side == 1)
        def _():
            for c, state in zip(blocks, states):
                keep(c, state)

    @pl.loop(0, near // 2)
    def _(m):
        blocks = (far_base + 2 * m, far_base + 2 * m + 1)
        for c in blocks:
            arrive(0, c)
        for c, state in zip(blocks, [prefix_step(c) for c in blocks]):
            keep(c, state)

        @pl.when(side == 0)
        def _():
            for c, state in zip(blocks, [half_step(c, 0, kept(c), split) for c in blocks]):
                keep(c, state)

    def last_step(m, count):
        first = (far_base + 2 * m) % n_blk
        blocks = (first, first + 1)
        finish(blocks, [half_step(c, 1 - side, kept(c), count) for c in blocks])

    for m in range(near):
        arrive(2, far_base + m)
        arrive(1, far_base + m)
        if m == 1:
            last_step(0, 2 * rows)

    @pl.loop(1, (1 + side) * (near // 2))
    def _(m):
        last_step(m, split)

    attn_in[b] = obuf[b]
    wo_copy.wait()

    def arrived(first, count):
        for m in range(count):

            @pl.when(first + m != b)
            def _():
                o_copy(0, first + m).wait_recv()

        return jnp.concatenate([attn_in[first + m] for m in range(count)], axis=1)

    def wo_rows(first, count):
        return pl.ds(pl.multiple_of(first * LANES, count * LANES), count * LANES)

    n_out = model // OUT_CHUNK

    def columns(j):
        return pl.ds(pl.multiple_of(j * OUT_CHUNK, OUT_CHUNK), OUT_CHUNK)

    near_rows, far_rows = wo_rows(near_base, near), wo_rows(far_base, near)
    attn[...] = arrived(near_base, near)

    @pl.loop(0, n_out)
    def _(j):
        low[:, columns(j)] = jnp.dot(
            attn[...], wobuf[near_rows, columns(j)], preferred_element_type=jnp.float32
        )

    attn[...] = arrived(far_base, near)

    share = rows // 2
    mine_rows = pl.ds(pl.multiple_of(t * share, share), share)
    other_rows = pl.ds(pl.multiple_of((1 - t) * share, share), share)

    def part_copy(j):
        return pltpu.make_async_remote_copy(
            part.at[j, other_rows, :],
            part_other.at[j],
            part_send.at[j],
            part_recv.at[j],
            device_id=partner,
            device_id_type=MESH,
        )

    @pl.loop(0, n_out)
    def _(j):
        product = low[:, columns(j)] + jnp.dot(
            attn[...], wobuf[far_rows, columns(j)], preferred_element_type=jnp.float32
        )
        part[j] = product.astype(jnp.bfloat16)
        part_copy(j).start()

    for j in range(n_out):
        part_copy(j).wait_recv()
        out_ref[:, j * OUT_CHUNK : (j + 1) * OUT_CHUNK] = (
            part[j, mine_rows, :].astype(jnp.float32) + part_other[j].astype(jnp.float32)
        ).astype(jnp.bfloat16)

    for j in range(n_out):
        part_copy(j).wait_send()
    for n in range(n_blk):

        if n < n_blk - 1:
            for c in range(3):
                qkv_copy(c, n, b).wait_send()
            o_copy(dest(n), b).wait_send()
        forward_copy(n, my_slot).wait_send()
    for n in range(n_blk - 1):
        seg_copy(n, b).wait_send()
        pre_copy(n, my_slot).wait_send()


def on_device_heads(hidden_in, norm_gain, w_qkv, w_out, prefix_kv, segment):
    rows, half = hidden_in.shape
    model = 2 * half
    width = w_qkv.shape[2]
    n_blk = width // LANES
    tokens = n_blk * rows
    pre_rows = prefix_kv.shape[0]
    rotated = HD // 4
    inverse = 10000.0 ** (-(np.arange(rotated // 2) * 2.0) / rotated)
    inverse = jnp.asarray(np.tile(inverse, (8, LANES // (rotated // 2))), jnp.float32)
    vmem = pl.BlockSpec(memory_space=pltpu.VMEM)
    hbm = pl.BlockSpec(memory_space=pl.ANY)
    bf16, f32 = jnp.bfloat16, jnp.float32
    dma = pltpu.SemaphoreType.DMA
    n_out = model // OUT_CHUNK

    def kernel(*refs):
        block_kernel(n_blk, *refs)

    attended, stacked = pl.pallas_call(
        kernel,
        name="attention_block",
        out_shape=(
            pltpu.VMEM((rows // 2, model), bf16),
            pltpu.VMEM((rows, 2, width), bf16),
        ),
        in_specs=[hbm, vmem, hbm, hbm, hbm, vmem, vmem],
        out_specs=(vmem, vmem),
        scratch_shapes=[
            pltpu.VMEM((n_blk // 2, 3, model, 2 * LANES), bf16),
            pltpu.VMEM((width, model), bf16),
            pltpu.VMEM((rows, half), bf16),
            pltpu.VMEM((rows, half), bf16),
            pltpu.VMEM((pre_rows, 2, width), bf16),
            pltpu.VMEM((rows, model), bf16),
            pltpu.VMEM((n_blk, 2, pre_rows, LANES), bf16),
            pltpu.VMEM((2, 2 * n_blk * pre_rows, LANES), bf16),
            pltpu.VMEM((8, rows), jnp.int32),
            pltpu.VMEM((n_blk, 8, rows), jnp.int32),
            pltpu.VMEM((8, tokens), f32),
            pltpu.VMEM((n_blk, rows, rows), f32),
            pltpu.VMEM((n_blk, 3, rows, LANES), bf16),
            pltpu.VMEM((3, tokens, LANES), bf16),
            pltpu.VMEM((n_blk, 2 * rows, 1), f32),
            pltpu.VMEM((n_blk, 2 * rows, 1), f32),
            pltpu.VMEM((n_blk, 2 * rows, LANES), f32),
            pltpu.VMEM((n_blk, rows, LANES), bf16),
            pltpu.VMEM((n_blk, rows, LANES), bf16),
            pltpu.VMEM((rows, width // 2), bf16),
            pltpu.VMEM((rows, model), f32),
            pltpu.VMEM((n_out, rows, OUT_CHUNK), bf16),
            pltpu.VMEM((n_out, rows // 2, OUT_CHUNK), bf16),
            dma((2,)),
            dma((3 * n_blk // 2,)),
            dma,
            dma((2,)),
            dma((n_blk,)),
            dma((n_blk,)),
            dma((2 * n_blk,)),
            dma((2 * n_blk,)),
            dma((3 * n_blk,)),
            dma((3 * n_blk,)),
            dma((n_blk,)),
            dma((n_blk,)),
            dma((n_out,)),
            dma((n_out,)),
        ],
        compiler_params=pltpu.CompilerParams(
            collective_id=0, has_side_effects=True, vmem_limit_bytes=56 * 1024 * 1024
        ),
    )(
        hidden_in,
        norm_gain[None, :],
        jnp.transpose(w_qkv, (1, 0, 2)),
        w_out,
        prefix_kv,
        segment,
        inverse,
    )
    return deliver(attended, stacked)


def deliver_kernel(attended_ref, stacked_ref, out_ref, kv_ref, sem):
    copies = []
    for n, (source, target) in enumerate(((stacked_ref, kv_ref), (attended_ref, out_ref))):
        share = source.shape[0] // DELIVER
        for i in range(DELIVER):
            part = pl.ds(i * share, share)
            copy = pltpu.make_async_copy(source.at[part], target.at[part], sem.at[n, i])
            copy.start()
            copies.append(copy)
    for copy in copies:
        copy.wait()


def deliver(attended, stacked):
    anywhere = pl.BlockSpec(memory_space=pl.ANY)
    inside = pl.BlockSpec(memory_space=pltpu.VMEM)
    return pl.pallas_call(
        deliver_kernel,
        name="deliver",
        out_shape=(
            jax.ShapeDtypeStruct(attended.shape, attended.dtype),
            jax.ShapeDtypeStruct(stacked.shape, stacked.dtype),
        ),
        in_specs=[inside, inside],
        out_specs=(anywhere, anywhere),
        scratch_shapes=[pltpu.SemaphoreType.DMA((2, DELIVER))],
    )(
        pltpu.with_memory_space_constraint(attended, pltpu.VMEM),
        pltpu.with_memory_space_constraint(stacked, pltpu.VMEM),
    )


def by_heads(hidden_in, norm_gain, w_qkv, w_out, prefix_kv, segment):
    rows, half = hidden_in.shape
    n_blk = lax.axis_size("blk")
    fits = (
        lax.axis_size("grp") == 2
        and lax.axis_size("tp") == 2
        and n_blk == 8
        and w_qkv.shape[2] == n_blk * LANES
        and rows == LANES
        and half % OUT_CHUNK == 0
        and prefix_kv.shape[0] % 16 == 0
    )
    form = on_device_heads if fits else on_device
    return form(hidden_in, norm_gain, w_qkv, w_out, prefix_kv, segment)


def solution(mesh):
    placed = (
        P(("grp", "blk"), "tp"),
        P(),
        P(None, None, "tp"),
        P("tp", None),
        P(("grp", "blk"), None, "tp"),
        P("grp", "blk"),
    )
    return jax.shard_map(
        by_heads,
        mesh=mesh,
        in_specs=placed,
        out_specs=(P(("grp", "blk", "tp"), None), P(("grp", "blk"), None, "tp")),
        check_vma=False,
    )
```

```python
import math

import jax
import jax.numpy as jnp
import numpy as np
from jax import lax
from jax.experimental import pallas as pl
from jax.experimental.pallas import tpu as pltpu
from jax.sharding import PartitionSpec as P

HD = 64
REQS = 8


def layer_norm(matrix_rows, norm_gain):
    values_f = matrix_rows.astype(jnp.float32)
    row_mean = jnp.mean(values_f, axis=-1, keepdims=True)
    centered = values_f - row_mean
    variance = jnp.mean(centered * centered, axis=-1, keepdims=True)
    return (centered * lax.rsqrt(variance + 1e-05) * norm_gain).astype(jnp.bfloat16)


def rotary(heads_f, positions):
    head_size = heads_f.shape[-1]
    rotated = head_size // 4
    half_rot = rotated // 2
    inverse = 10000.0 ** (-(jnp.arange(half_rot, dtype=jnp.float32) * 2.0) / rotated)
    angles = positions[:, None] * inverse[None, :]
    cos_table = jnp.cos(angles)[:, None, :]
    sine_table = jnp.sin(angles)[:, None, :]
    first_half = heads_f[..., :half_rot]
    second_half = heads_f[..., half_rot:rotated]
    return jnp.concatenate(
        [
            first_half * cos_table - second_half * sine_table,
            second_half * cos_table + first_half * sine_table,
            heads_f[..., rotated:],
        ],
        axis=-1,
    )


def attend_block(carried, queries, block_kv, visible, score_scale):
    maxima, totals, accumulated = carried
    key_count = block_kv.shape[0]
    head_count = queries.shape[1]
    block_keys = block_kv[:, 0].reshape(key_count, head_count, HD)
    block_values = block_kv[:, 1].reshape(key_count, head_count, HD)
    scores = (
        jnp.einsum("qhd,khd->qhk", queries, block_keys, preferred_element_type=jnp.float32)
        * score_scale
    )
    if visible is not None:
        scores = jnp.where(visible[:, None, :], scores, jnp.float32(-1e30))
    newest = jnp.maximum(maxima, jnp.max(scores, axis=-1))
    weights = jnp.exp(scores - newest[..., None])
    if visible is not None:
        weights = jnp.where(visible[:, None, :], weights, jnp.float32(0.0))
    factor = jnp.exp(maxima - newest)
    totals = totals * factor + jnp.sum(weights, axis=-1)
    accumulated = accumulated * factor[..., None] + jnp.einsum(
        "qhk,khd->qhd",
        weights.astype(jnp.bfloat16),
        block_values,
        preferred_element_type=jnp.float32,
    )
    return (newest, totals, accumulated)


def on_device(hidden_in, norm_gain, w_qkv, w_out, prefix_kv, segment):
    row_count = hidden_in.shape[0]
    local_width = w_qkv.shape[2]
    head_count = local_width // HD
    gathered = lax.all_gather(hidden_in, "tp", axis=1, tiled=True)
    normed = layer_norm(gathered, norm_gain)
    projected = jnp.einsum("td,dce->tce", normed, w_qkv, preferred_element_type=jnp.float32)
    seg_row = segment[0]
    labels = jnp.arange(REQS, dtype=jnp.int32)
    onehot = (seg_row[:, None] == labels[None, :]).astype(jnp.int32)
    counts = jnp.sum(onehot, axis=0)
    all_counts = lax.all_gather(counts[None, :], "blk", axis=0, tiled=True)
    request_sizes = jnp.sum(all_counts, axis=0)
    request_ends = jnp.sum(
        jnp.where(labels[None, :] <= labels[:, None], request_sizes[None, :], 0), axis=1
    )
    request_starts = request_ends - request_sizes
    cycle_size = lax.axis_size("blk")
    cycle_place = lax.axis_index("blk")
    row_index = jnp.arange(row_count, dtype=jnp.int32)
    query_index = cycle_place * row_count + row_index
    within = query_index - jnp.sum(onehot * request_starts[None, :], axis=1)
    prefix_len = prefix_kv.shape[0] * lax.axis_size("grp") * cycle_size
    positions = within.astype(jnp.float32) + float(prefix_len)
    queries = rotary(projected[:, 0].reshape(row_count, head_count, HD), positions).astype(
        jnp.bfloat16
    )
    key_heads = rotary(projected[:, 1].reshape(row_count, head_count, HD), positions).astype(
        jnp.bfloat16
    )
    values = projected[:, 2].astype(jnp.bfloat16)
    keys_values = jnp.stack([key_heads.reshape(row_count, local_width), values], axis=1)
    score_scale = 1.0 / math.sqrt(HD)
    running = (
        jnp.full((row_count, head_count), -1e30, jnp.float32),
        jnp.zeros((row_count, head_count), jnp.float32),
        jnp.zeros((row_count, head_count, HD), jnp.float32),
    )
    running = attend_block(
        running,
        queries,
        lax.all_gather(prefix_kv, ("grp", "blk"), axis=0, tiled=True),
        None,
        score_scale,
    )
    block_kv = lax.all_gather(keys_values, "blk", axis=0, tiled=True)
    key_index = jnp.arange(block_kv.shape[0], dtype=jnp.int32)
    key_segment = jnp.sum((key_index[:, None] >= request_ends[None, :]).astype(jnp.int32), axis=1)
    visible = (
        (key_segment[None, :] == seg_row[:, None])
        & (key_index[None, :] <= query_index[:, None])
        & True
    )

    def take_block(kept):
        return attend_block(kept, queries, block_kv, visible, score_scale)

    def skip_block(kept):
        return kept

    running = lax.cond(jnp.any(visible), take_block, skip_block, running)
    maxima, totals, accumulated = running
    attention = (
        (accumulated / totals[..., None]).astype(jnp.bfloat16).reshape(row_count, local_width)
    )
    attended = lax.psum_scatter(
        jnp.dot(attention, w_out, preferred_element_type=jnp.float32).astype(jnp.bfloat16),
        "tp",
        scatter_dimension=0,
        tiled=True,
    )
    return (attended, keys_values)


LANES = 128
OUT_CHUNK = 512
DELIVER = 2
MESH = pl.DeviceIdType.MESH


def head_pairs(block):
    wide = block.astype(jnp.float32)
    lane = lax.broadcasted_iota(jnp.int32, wide.shape, 1)
    first = jnp.where(lane < HD, wide, 0.0)
    second = jnp.where(lane < HD, 0.0, wide)
    return jnp.concatenate([first, second], axis=0).astype(jnp.bfloat16)


def attend_step(stacked, keys, values, mask, state):
    factor = math.log2(math.e) / math.sqrt(HD)
    scores = lax.dot_general(
        stacked, keys, (((1,), (1,)), ((), ())), preferred_element_type=jnp.float32
    )
    if mask is not None:
        rows = mask.shape[0]
        scores = jnp.concatenate(
            [
                jnp.where(mask, scores[:rows], jnp.float32(-1e30)),
                jnp.where(mask, scores[rows:], jnp.float32(-1e30)),
            ],
            axis=0,
        )
    top = jnp.max(scores, axis=1, keepdims=True)
    if state is not None:
        top = jnp.maximum(top, state[0])
    weights = jnp.exp2((scores - top) * factor)
    total = jnp.sum(weights, axis=1, keepdims=True)
    summed = jnp.dot(weights.astype(jnp.bfloat16), values, preferred_element_type=jnp.float32)
    if state is not None:
        shrink = jnp.exp2((state[0] - top) * factor)
        total = total + state[1] * shrink
        summed = summed + state[2] * shrink
    return top, total, summed


def block_kernel(
    n_blk,
    hid_ref,
    gain_ref,
    w_ref,
    wo_ref,
    pre_ref,
    seg_ref,
    inv_ref,
    out_ref,
    kv_ref,
    wbuf,
    wobuf,
    hid_mine,
    hid_other,
    pre_mine,
    normed,
    pre_out,
    pre_all,
    seg_out,
    seg_all,
    seg_flat,
    seg_col,
    send_buf,
    qkv,
    top_s,
    total_s,
    sum_s,
    obuf,
    attn_in,
    attn,
    low,
    part,
    part_other,
    in_sem,
    w_sem,
    wo_sem,
    hid_sem,
    seg_send,
    seg_recv,
    pre_send,
    pre_recv,
    qkv_send,
    qkv_recv,
    o_send,
    o_recv,
    part_send,
    part_recv,
):
    g, b, t = lax.axis_index("grp"), lax.axis_index("blk"), lax.axis_index("tp")
    rows, half = hid_mine.shape
    model = 2 * half
    pre_rows = pre_mine.shape[0]
    n_z = n_blk // 2
    near = n_blk // 2
    z, x = b // 2, b % 2
    side = z // 2
    near_base, far_base = side * near, (1 - side) * near
    partner = (g, b, 1 - t)
    across = (1 - g, b, t)

    def dest_z(i):
        if i < 2:
            return (1 - side) * (n_z - 1 - i) + side * i
        return side * 2 + (z % 2 + n_z - 1 - i) % 2

    def dest(n):
        return dest_z(n // 2) * 2 + (x + 1 + n) % 2

    def lanes(block):
        return pl.ds(pl.multiple_of(block * LANES, LANES), LANES)

    def token_rows(block):
        return pl.ds(pl.multiple_of(block * rows, rows), rows)

    barrier = pltpu.get_barrier_semaphore()
    pl.semaphore_signal(barrier, inc=1, device_id=partner, device_id_type=MESH)
    pl.semaphore_signal(barrier, inc=1, device_id=across, device_id_type=MESH)
    for n in range(n_blk - 1):
        pl.semaphore_signal(barrier, inc=1, device_id=(g, dest(n), t), device_id_type=MESH)

    pre_load = pltpu.make_async_copy(pre_ref, pre_mine, in_sem.at[0])
    pre_load.start()
    hid_load = pltpu.make_async_copy(hid_ref, hid_mine, in_sem.at[1])
    hid_load.start()
    pre_load.wait()
    hid_load.wait()

    def w_cols(i):
        return pl.ds(pl.multiple_of(dest_z(i) * 2 * LANES, 2 * LANES), 2 * LANES)

    def w_load(c, i):
        return pltpu.make_async_copy(
            w_ref.at[c, :, w_cols(i)], wbuf.at[i, c], w_sem.at[c * n_z + i]
        )

    for c in (2, 0, 1):
        for i in range(n_z):
            w_load(c, (i + 2 * (c % 2)) % n_z).start()
    wo_copy = pltpu.make_async_copy(wo_ref, wobuf, wo_sem)
    wo_copy.start()

    seg_out[...] = jnp.broadcast_to(seg_ref[...], seg_out.shape)
    for d in range(n_blk):
        for c in range(2):
            pre_out[d, c] = pre_mine[:, c, d * LANES : (d + 1) * LANES]
    pl.semaphore_wait(barrier, n_blk + 1)

    hid_copy = pltpu.make_async_remote_copy(
        hid_mine, hid_other, hid_sem.at[0], hid_sem.at[1], device_id=partner, device_id_type=MESH
    )
    hid_copy.start()

    def seg_copy(n, slot):
        return pltpu.make_async_remote_copy(
            seg_out,
            seg_all.at[slot],
            seg_send.at[n],
            seg_recv.at[slot],
            device_id=(g, dest(n), t),
            device_id_type=MESH,
        )

    for n in range(n_blk - 1):
        seg_copy(n, b).start()

    def pre_slot(slot):
        return pre_all.at[:, pl.ds(pl.multiple_of(slot * pre_rows, pre_rows), pre_rows), :]

    def pre_copy(n, slot):
        return pltpu.make_async_remote_copy(
            pre_out.at[dest(n)],
            pre_slot(slot),
            pre_send.at[n],
            pre_recv.at[slot],
            device_id=(g, dest(n), t),
            device_id_type=MESH,
        )

    def forward_copy(n, slot):
        return pltpu.make_async_remote_copy(
            pre_slot(slot),
            pre_slot(slot),
            pre_send.at[n_blk + n],
            pre_recv.at[slot],
            device_id=across,
            device_id_type=MESH,
        )

    my_slot = g * n_blk + b
    for n in range(n_blk - 1):
        pre_copy(n, my_slot).start()
    pre_all[:, pl.ds(pl.multiple_of(my_slot * pre_rows, pre_rows), pre_rows), :] = pre_out[b]
    forward_copy(n_blk - 1, my_slot).start()
    seg_all[b] = seg_out[...]

    def pass_on(numbers):
        for n in numbers:
            slot = g * n_blk + dest(n)
            pre_copy(n, slot).wait_recv()
            forward_copy(n, slot).start()

    mine = hid_mine[...].astype(jnp.float32)
    mine_sum = jnp.sum(mine, axis=1, keepdims=True)
    hid_copy.wait()
    other = hid_other[...].astype(jnp.float32)
    mean = (mine_sum + jnp.sum(other, axis=1, keepdims=True)) * (1.0 / model)
    mine = mine - mean
    other = other - mean
    variance = (
        jnp.sum(mine * mine, axis=1, keepdims=True)
        + jnp.sum(other * other, axis=1, keepdims=True)
    ) * (1.0 / model)
    scale = lax.rsqrt(variance + 1e-05)
    mine_cols = pl.ds(pl.multiple_of(t * half, half), half)
    other_cols = pl.ds(pl.multiple_of((1 - t) * half, half), half)
    normed[:, mine_cols] = (mine * scale * gain_ref[:, mine_cols]).astype(jnp.bfloat16)
    normed[:, other_cols] = (other * scale * gain_ref[:, other_cols]).astype(jnp.bfloat16)

    def qkv_copy(c, n, slot):
        return pltpu.make_async_remote_copy(
            send_buf.at[n, c],
            qkv.at[c, token_rows(slot), :],
            qkv_send.at[c * n_blk + n],
            qkv_recv.at[c * n_blk + slot],
            device_id=(g, dest(n), t),
            device_id_type=MESH,
        )

    def start_others(c, i):
        for n in (2 * i, 2 * i + 1):
            if n < n_blk - 1:
                qkv_copy(c, n, b).start()

    for i in range(n_z):
        w_load(2, i).wait()
        product = jnp.dot(normed[...], wbuf[i, 2], preferred_element_type=jnp.float32)
        for h in range(2):
            tile = product[:, h * LANES : (h + 1) * LANES].astype(jnp.bfloat16)
            send_buf[2 * i + (x + 1 + h) % 2, 2] = tile
            kv_ref[:, 1, lanes(dest_z(i) * 2 + h)] = tile
        start_others(2, i)

    for n in range(n_blk - 1):
        seg_copy(n, dest(n)).wait_recv()
    for c in range(n_blk):
        row = seg_all[c].astype(jnp.float32)
        seg_flat[:, c * rows : (c + 1) * rows] = row
        seg_col[c] = jnp.broadcast_to(row[:1], (rows, rows)).T
    own_seg = seg_col[b][:, :1]
    before = jnp.where(seg_flat[:1] < own_seg, 1.0, 0.0)
    start = jnp.sum(before, axis=1, keepdims=True)
    row_iota = lax.broadcasted_iota(jnp.int32, (rows, LANES), 0)
    prefix_len = float(2 * n_blk * pre_rows)
    position = (b * rows + row_iota).astype(jnp.float32) - start + prefix_len
    angles = position * inv_ref[:1]
    in_head = lax.broadcasted_iota(jnp.int32, (rows, LANES), 1) % HD
    rotated = HD // 4
    sine = jnp.sin(angles)
    cos_t = jnp.where(in_head < rotated, jnp.cos(angles), 1.0)
    low_t = jnp.where(in_head < rotated // 2, -sine, 0.0)
    high_t = jnp.where((in_head >= rotated // 2) & (in_head < rotated), sine, 0.0)


    for m in range(2 * n_z):
        c = m // n_z
        i = m % n_z if c == 0 else (m + 2) % n_z
        w_load(c, i).wait()
        product = jnp.dot(normed[...], wbuf[i, c], preferred_element_type=jnp.float32)
        for h in range(2):
            tile = product[:, h * LANES : (h + 1) * LANES]
            tile = (
                tile * cos_t
                + pltpu.roll(tile, LANES - rotated // 2, 1) * low_t
                + pltpu.roll(tile, rotated // 2, 1) * high_t
            ).astype(jnp.bfloat16)
            send_buf[2 * i + (x + 1 + h) % 2, c] = tile
            if c == 1:
                kv_ref[:, 0, lanes(dest_z(i) * 2 + h)] = tile
        if c == 0 or i != 1:
            start_others(c, i)

    qkv[:, token_rows(b), :] = send_buf[n_blk - 1]
    pass_on((6, 5, 4, 3, 2, 1, 0))

    for c in range(n_blk):
        forward_copy(c, (1 - g) * n_blk + c).wait_recv()

    split = near * rows

    def o_copy(block, slot):
        return pltpu.make_async_remote_copy(
            obuf.at[block],
            attn_in.at[slot],
            o_send.at[block],
            o_recv.at[slot],
            device_id=(g, block, t),
            device_id_type=MESH,
        )

    def arrive(c, block):
        qkv_copy(c, 0, block).wait_recv()

    def queries(block):
        return head_pairs(qkv[0, token_rows(block), :])

    def prefix_step(block):
        return attend_step(queries(block), pre_all[0], pre_all[1], None, None)

    def half_step(block, c, state, count):
        q_seg = seg_col[block][:, :1]
        q_index = block * rows + lax.broadcasted_iota(jnp.int32, (rows, count), 0)
        k_index = c * split + lax.broadcasted_iota(jnp.int32, (rows, count), 1)
        keys = pl.ds(pl.multiple_of(c * split, split), count)
        mask = (seg_flat[pl.ds(0, 1), keys] == q_seg) & (k_index <= q_index)
        return attend_step(queries(block), qkv[1, keys, :], qkv[2, keys, :], mask, state)

    def keep(block, state):
        top_s[block], total_s[block], sum_s[block] = state

    def kept(block):
        return top_s[block], total_s[block], sum_s[block]

    def finish(blocks, states):
        lane = lax.broadcasted_iota(jnp.int32, (rows, LANES), 1)
        for block, (_, total, summed) in zip(blocks, states):
            result = summed / total
            obuf[block] = jnp.where(lane < HD, result[:rows], result[rows:]).astype(jnp.bfloat16)
        for block in blocks:

            @pl.when(block != b)
            def _():
                o_copy(block, b).start()

    for n in range(near, n_blk - 1):
        for c in range(3):
            arrive(c, dest(n))

    @pl.loop(0, near // 2)
    def _(m):
        @pl.when(m == 1)
        def _():
            start_others(1, 1)

        blocks = (near_base + 2 * m, near_base + 2 * m + 1)
        states = [half_step(c, side, prefix_step(c), split) for c in blocks]

        @pl.when(side == 0)
        def _():
            finish(blocks, states)

        @pl.when(side == 1)
        def _():
            for c, state in zip(blocks, states):
                keep(c, state)

    @pl.loop(0, near // 2)
    def _(m):
        blocks = (far_base + 2 * m, far_base + 2 * m + 1)
        for c in blocks:
            arrive(0, c)
        for c, state in zip(blocks, [prefix_step(c) for c in blocks]):
            keep(c, state)

        @pl.when(side == 0)
        def _():
            for c, state in zip(blocks, [half_step(c, 0, kept(c), split) for c in blocks]):
                keep(c, state)

    def last_step(m, count):
        first = (far_base + 2 * m) % n_blk
        blocks = (first, first + 1)
        finish(blocks, [half_step(c, 1 - side, kept(c), count) for c in blocks])

    for m in range(near):
        arrive(2, far_base + m)
        arrive(1, far_base + m)
        if m == 1:
            last_step(0, 2 * rows)

    @pl.loop(1, (1 + side) * (near // 2))
    def _(m):
        last_step(m, split)

    attn_in[b] = obuf[b]
    wo_copy.wait()

    def arrived(first, count):
        for m in range(count):

            @pl.when(first + m != b)
            def _():
                o_copy(0, first + m).wait_recv()

        return jnp.concatenate([attn_in[first + m] for m in range(count)], axis=1)

    def wo_rows(first, count):
        return pl.ds(pl.multiple_of(first * LANES, count * LANES), count * LANES)

    n_out = model // OUT_CHUNK

    def columns(j):
        return pl.ds(pl.multiple_of(j * OUT_CHUNK, OUT_CHUNK), OUT_CHUNK)

    early, late = dest_z(0) * 2, dest_z(1) * 2
    near_rows = wo_rows(near_base, near)
    early_rows, late_rows = wo_rows(early, 2), wo_rows(late, 2)
    attn[...] = arrived(near_base, near)

    @pl.loop(0, n_out)
    def _(j):
        low[:, columns(j)] = jnp.dot(
            attn[...], wobuf[near_rows, columns(j)], preferred_element_type=jnp.float32
        )

    attn[:, : 2 * LANES] = arrived(early, 2)

    @pl.loop(0, n_out)
    def _(j):
        low[:, columns(j)] += jnp.dot(
            attn[:, : 2 * LANES],
            wobuf[early_rows, columns(j)],
            preferred_element_type=jnp.float32,
        )

    attn[:, : 2 * LANES] = arrived(late, 2)

    share = rows // 2
    mine_rows = pl.ds(pl.multiple_of(t * share, share), share)
    other_rows = pl.ds(pl.multiple_of((1 - t) * share, share), share)

    def part_copy(j):
        return pltpu.make_async_remote_copy(
            part.at[j, other_rows, :],
            part_other.at[j],
            part_send.at[j],
            part_recv.at[j],
            device_id=partner,
            device_id_type=MESH,
        )

    @pl.loop(0, n_out)
    def _(j):
        product = low[:, columns(j)] + jnp.dot(
            attn[:, : 2 * LANES],
            wobuf[late_rows, columns(j)],
            preferred_element_type=jnp.float32,
        )
        part[j] = product.astype(jnp.bfloat16)
        part_copy(j).start()

    for j in range(n_out):
        part_copy(j).wait_recv()
        out_ref[:, j * OUT_CHUNK : (j + 1) * OUT_CHUNK] = (
            part[j, mine_rows, :].astype(jnp.float32) + part_other[j].astype(jnp.float32)
        ).astype(jnp.bfloat16)

    for j in range(n_out):
        part_copy(j).wait_send()
    for n in range(n_blk):

        if n < n_blk - 1:
            for c in range(3):
                qkv_copy(c, n, b).wait_send()
            o_copy(dest(n), b).wait_send()
        forward_copy(n, my_slot).wait_send()
    for n in range(n_blk - 1):
        seg_copy(n, b).wait_send()
        pre_copy(n, my_slot).wait_send()


def on_device_heads(hidden_in, norm_gain, w_qkv, w_out, prefix_kv, segment):
    rows, half = hidden_in.shape
    model = 2 * half
    width = w_qkv.shape[2]
    n_blk = width // LANES
    tokens = n_blk * rows
    pre_rows = prefix_kv.shape[0]
    rotated = HD // 4
    inverse = 10000.0 ** (-(np.arange(rotated // 2) * 2.0) / rotated)
    inverse = jnp.asarray(np.tile(inverse, (8, LANES // (rotated // 2))), jnp.float32)
    vmem = pl.BlockSpec(memory_space=pltpu.VMEM)
    hbm = pl.BlockSpec(memory_space=pl.ANY)
    bf16, f32 = jnp.bfloat16, jnp.float32
    dma = pltpu.SemaphoreType.DMA
    n_out = model // OUT_CHUNK

    def kernel(*refs):
        block_kernel(n_blk, *refs)

    attended, stacked = pl.pallas_call(
        kernel,
        name="attention_block",
        out_shape=(
            pltpu.VMEM((rows // 2, model), bf16),
            pltpu.VMEM((rows, 2, width), bf16),
        ),
        in_specs=[hbm, vmem, hbm, hbm, hbm, vmem, vmem],
        out_specs=(vmem, vmem),
        scratch_shapes=[
            pltpu.VMEM((n_blk // 2, 3, model, 2 * LANES), bf16),
            pltpu.VMEM((width, model), bf16),
            pltpu.VMEM((rows, half), bf16),
            pltpu.VMEM((rows, half), bf16),
            pltpu.VMEM((pre_rows, 2, width), bf16),
            pltpu.VMEM((rows, model), bf16),
            pltpu.VMEM((n_blk, 2, pre_rows, LANES), bf16),
            pltpu.VMEM((2, 2 * n_blk * pre_rows, LANES), bf16),
            pltpu.VMEM((8, rows), jnp.int32),
            pltpu.VMEM((n_blk, 8, rows), jnp.int32),
            pltpu.VMEM((8, tokens), f32),
            pltpu.VMEM((n_blk, rows, rows), f32),
            pltpu.VMEM((n_blk, 3, rows, LANES), bf16),
            pltpu.VMEM((3, tokens, LANES), bf16),
            pltpu.VMEM((n_blk, 2 * rows, 1), f32),
            pltpu.VMEM((n_blk, 2 * rows, 1), f32),
            pltpu.VMEM((n_blk, 2 * rows, LANES), f32),
            pltpu.VMEM((n_blk, rows, LANES), bf16),
            pltpu.VMEM((n_blk, rows, LANES), bf16),
            pltpu.VMEM((rows, width // 2), bf16),
            pltpu.VMEM((rows, model), f32),
            pltpu.VMEM((n_out, rows, OUT_CHUNK), bf16),
            pltpu.VMEM((n_out, rows // 2, OUT_CHUNK), bf16),
            dma((2,)),
            dma((3 * n_blk // 2,)),
            dma,
            dma((2,)),
            dma((n_blk,)),
            dma((n_blk,)),
            dma((2 * n_blk,)),
            dma((2 * n_blk,)),
            dma((3 * n_blk,)),
            dma((3 * n_blk,)),
            dma((n_blk,)),
            dma((n_blk,)),
            dma((n_out,)),
            dma((n_out,)),
        ],
        compiler_params=pltpu.CompilerParams(
            collective_id=0, has_side_effects=True, vmem_limit_bytes=56 * 1024 * 1024
        ),
    )(
        hidden_in,
        norm_gain[None, :],
        jnp.transpose(w_qkv, (1, 0, 2)),
        w_out,
        prefix_kv,
        segment,
        inverse,
    )
    return deliver(attended, stacked)


def deliver_kernel(attended_ref, stacked_ref, out_ref, kv_ref, sem):
    copies = []
    for n, (source, target) in enumerate(((stacked_ref, kv_ref), (attended_ref, out_ref))):
        share = source.shape[0] // DELIVER
        for i in range(DELIVER):
            part = pl.ds(i * share, share)
            copy = pltpu.make_async_copy(source.at[part], target.at[part], sem.at[n, i])
            copy.start()
            copies.append(copy)
    for copy in copies:
        copy.wait()


def deliver(attended, stacked):
    anywhere = pl.BlockSpec(memory_space=pl.ANY)
    inside = pl.BlockSpec(memory_space=pltpu.VMEM)
    return pl.pallas_call(
        deliver_kernel,
        name="deliver",
        out_shape=(
            jax.ShapeDtypeStruct(attended.shape, attended.dtype),
            jax.ShapeDtypeStruct(stacked.shape, stacked.dtype),
        ),
        in_specs=[inside, inside],
        out_specs=(anywhere, anywhere),
        scratch_shapes=[pltpu.SemaphoreType.DMA((2, DELIVER))],
    )(
        pltpu.with_memory_space_constraint(attended, pltpu.VMEM),
        pltpu.with_memory_space_constraint(stacked, pltpu.VMEM),
    )


def by_heads(hidden_in, norm_gain, w_qkv, w_out, prefix_kv, segment):
    rows, half = hidden_in.shape
    n_blk = lax.axis_size("blk")
    fits = (
        lax.axis_size("grp") == 2
        and lax.axis_size("tp") == 2
        and n_blk == 8
        and w_qkv.shape[2] == n_blk * LANES
        and rows == LANES
        and half % OUT_CHUNK == 0
        and prefix_kv.shape[0] % 16 == 0
    )
    form = on_device_heads if fits else on_device
    return form(hidden_in, norm_gain, w_qkv, w_out, prefix_kv, segment)


def solution(mesh):
    placed = (
        P(("grp", "blk"), "tp"),
        P(),
        P(None, None, "tp"),
        P("tp", None),
        P(("grp", "blk"), None, "tp"),
        P("grp", "blk"),
    )
    return jax.shard_map(
        by_heads,
        mesh=mesh,
        in_specs=placed,
        out_specs=(P(("grp", "blk", "tp"), None), P(("grp", "blk"), None, "tp")),
        check_vma=False,
    )
```
